256 devices in a mesh: gx: 16 (over z_lo, y, core), gy: 16 (over z_hi, x).
Axes of the slice: x: 4, y: 4, z: 8 (z_hi: 4, z_lo: 2; z = z_hi * 2 + z_lo), core: 2. Of those that a mesh axis runs over, the one named last changes fastest.
Arguments:
- state: float32 [286, 2, 32, 2048], P(None, None, 'gy', 'gx'), may hold values from -6 to 6
- adjoint: float32 [286, 2, 32, 2048], P(None, None, 'gy', 'gx'), may hold values from -6 to 6
- upwind_pos: float32 [3, 286, 286], replicated, may hold values from -0.375 to 0.375
- upwind_neg: float32 [3, 286, 286], replicated, may hold values from -0.375 to 0.375
- collision: float32 [35, 35, 35], replicated, may hold values from -0.15625 to 0.15625
- relax: float32 [286], replicated, may hold values from 0.1 to 2
- wall_table: float32 [3, 286], replicated, may hold values from 0 to 2
- drag_weights: float32 [286], replicated, may hold values from -6 to 6
- block_inverse: float32 [286, 286], replicated, may hold values from -0.375 to 0.375
- cell_codes: int32 [2, 32, 2048], P(None, 'gy', 'gx'), may hold values from 0 to 3
- wall_mask: int32 [2, 32, 2048], P(None, 'gy', 'gx'), may hold values 0 or 1
Outputs:
- state_next: float32 [286, 2, 32, 2048], P(None, None, 'gy', 'gx')
- adjoint_next: float32 [286, 2, 32, 2048], P(None, None, 'gy', 'gx')
The draws below stay inside these ranges and needn't reach their ends.
All inputs are finite; a program needn't handle non-finite values. No bound on the sum of `wall_mask` on one device may be relied on, other than what follows from the above.
Results may differ from the reference program's by a relative error of at most 0.0003.
Values sent between devices are 32-bit elements; how exact they have to be, the bound alone decides.
No kernel may reach another device: no remote copies, remote signals or barrier semaphores. Data moves between devices by JAX's collectives and lax.ppermute only.
A program may use at most 64 MiB of HBM per device.

```python
import math
import jax
import jax.numpy as jnp
from jax import lax

M = 286
MLOW = 35
PLANES = 2
NX = 2048
NY = 32


def place_ends(result, key, least, top_value):
    longest = result.shape.index(max(result.shape))
    spots = []
    for shift in (0, 1):
        where = [jax.random.randint(jax.random.fold_in(key, axis), (), 0, length) for axis, length in enumerate(result.shape)]
        where[longest] = (where[longest] + shift) % result.shape[longest]
        spots.append(tuple(where))
    return result.at[spots[0]].set(least).at[spots[1]].set(top_value)


def block_scale(rng, extent, pieces, low, largest):
    loudness, own = 1.0, jax.random.fold_in(rng, 6)
    for axis_at, blocks in pieces:
        draws = jnp.exp(jax.random.uniform(jax.random.fold_in(own, axis_at), (blocks,), jnp.float32, low / len(pieces), largest / len(pieces)))
        loudness = loudness * jnp.repeat(draws, extent[axis_at] // blocks).reshape([-1 if axis == axis_at else 1 for axis in range(len(extent))])
    return loudness


def normal_values(rng, extent, spread, most, shards=(), kind=jnp.bfloat16):
    drawn = spread * jax.random.normal(rng, extent, jnp.float32)
    if shards:
        drawn = drawn * block_scale(rng, extent, shards, -0.22, 0.18)
    return jnp.clip(drawn, -most, most).astype(kind)


def setup_inputs(seed: int = 0) -> dict:
    streams_of = jax.random.split(jax.random.key(seed), 12)
    return {
        "state": normal_values(streams_of[0], (M, PLANES, NY, NX), 1.0, 6.0, ((2, 16), (3, 16)), jnp.float32),
        "adjoint": normal_values(streams_of[1], (M, PLANES, NY, NX), 1.0, 6.0, ((2, 16), (3, 16)), jnp.float32),
        "upwind_pos": normal_values(streams_of[2], (3, M, M), M ** -0.5, 0.375, (), jnp.float32),
        "upwind_neg": normal_values(streams_of[3], (3, M, M), M ** -0.5, 0.375, (), jnp.float32),
        "collision": normal_values(streams_of[4], (MLOW, MLOW, MLOW), (MLOW * MLOW) ** -0.5, 0.15625, (), jnp.float32),
        "relax": jnp.clip(jnp.exp(jax.random.uniform(streams_of[5], (M,), jnp.float32, math.log(0.1), math.log(2.0))), 0.1, 2.0),
        "wall_table": jnp.clip(jax.random.uniform(streams_of[6], (3, M), jnp.float32, 0.0, 2.0), 0.0, 2.0),
        "drag_weights": normal_values(streams_of[7], (M,), 1.0, 6.0, (), jnp.float32),
        "block_inverse": normal_values(streams_of[8], (M, M), M ** -0.5, 0.375, (), jnp.float32),
        "cell_codes": place_ends(jax.random.randint(streams_of[9], (PLANES, NY, NX), 0, 4), jax.random.fold_in(streams_of[9], 1), 0, 3).astype(jnp.int32),
        "wall_mask": place_ends((jax.random.randint(streams_of[10], (PLANES, NY, NX), 0, 4) < 1).astype(jnp.int32), jax.random.fold_in(streams_of[10], 1), 0, 1),
    }


def apply_matrix(matrix, field):
    return jnp.dot(matrix, field, precision=lax.Precision.HIGHEST)


def reference(state, adjoint, upwind_pos, upwind_neg, collision, relax, wall_table, drag_weights, block_inverse, cell_codes, wall_mask):
    moments = state.shape[0]
    depth = state.shape[1]
    height = state.shape[2]
    width = state.shape[3]
    lowest = collision.shape[0]
    flat_gain = collision.reshape(lowest, lowest * lowest)
    symmetric = collision + jnp.transpose(collision, (0, 2, 1))
    flat_adgain = jnp.transpose(symmetric, (1, 0, 2)).reshape(lowest, lowest * lowest)

    def take_row(field, zpos, ypos):
        valid = jnp.logical_and(ypos >= 0, ypos < height)
        yclip = jnp.clip(ypos, 0, height - 1).astype(jnp.int32)
        start = (jnp.int32(0), zpos.astype(jnp.int32), yclip, jnp.int32(0))
        row = lax.dynamic_slice(field, start, (moments, 1, 1, width)).reshape(moments, width)
        return jnp.where(valid, row, jnp.zeros_like(row))

    def one_row(index):
        zplane = index // height
        yrow = index % height
        zlow = (zplane + depth - 1) % depth
        zhigh = (zplane + 1) % depth
        results = []
        for field, is_adjoint in ((state, False), (adjoint, True)):
            center = take_row(field, zplane, yrow)
            xminus = jnp.pad(center, ((0, 0), (1, 0)))[:, :-1]
            xplus = jnp.pad(center, ((0, 0), (0, 1)))[:, 1:]
            yminus = take_row(field, zplane, yrow - 1)
            yplus = take_row(field, zplane, yrow + 1)
            zminus = take_row(field, zlow, yrow)
            zplus = take_row(field, zhigh, yrow)
            minus_all = (xminus, yminus, zminus)
            plus_all = (xplus, yplus, zplus)
            total = jnp.zeros_like(center)
            for direction in range(3):
                if is_adjoint:
                    total = total + apply_matrix(upwind_pos[direction].T, center - plus_all[direction])
                    total = total + apply_matrix(upwind_neg[direction].T, minus_all[direction] - center)
                else:
                    total = total + apply_matrix(upwind_pos[direction], center - minus_all[direction])
                    total = total + apply_matrix(upwind_neg[direction], plus_all[direction] - center)
            results.append((center, total))
        (state_row, stream), (adjoint_row, adstream) = results
        codes = lax.dynamic_slice(cell_codes, (zplane.astype(jnp.int32), yrow.astype(jnp.int32), jnp.int32(0)), (1, 1, width)).reshape(width)
        walls = lax.dynamic_slice(wall_mask, (zplane.astype(jnp.int32), yrow.astype(jnp.int32), jnp.int32(0)), (1, 1, width)).reshape(width)
        onehot = (codes[None, :] == jnp.arange(1, 4, dtype=jnp.int32)[:, None]).astype(state.dtype)
        damp = relax[:, None] + apply_matrix(wall_table.T, onehot)
        state_low = state_row[:lowest]
        adjoint_low = adjoint_row[:lowest]
        products = (state_low[:, None, :] * state_low[None, :, :]).reshape(lowest * lowest, width)
        gain = jnp.pad(apply_matrix(flat_gain, products), ((0, moments - lowest), (0, 0)))
        cross = (adjoint_low[:, None, :] * state_low[None, :, :]).reshape(lowest * lowest, width)
        adgain = jnp.pad(apply_matrix(flat_adgain, cross), ((0, moments - lowest), (0, 0)))
        primal_res = stream - gain + damp * state_row
        state_new = state_row - 0.5 * apply_matrix(block_inverse, primal_res)
        adjoint_res = adstream - adgain + damp * adjoint_row - walls.astype(state.dtype)[None, :] * drag_weights[:, None]
        adjoint_new = adjoint_row - 0.5 * apply_matrix(block_inverse.T, adjoint_res)
        return state_new, adjoint_new

    rows_state, rows_adjoint = lax.map(one_row, jnp.arange(depth * height, dtype=jnp.int32))
    state_next = jnp.transpose(rows_state.reshape(depth, height, moments, width), (2, 0, 1, 3))
    adjoint_next = jnp.transpose(rows_adjoint.reshape(depth, height, moments, width), (2, 0, 1, 3))
    return state_next, adjoint_next
```

```python
import jax
import jax.numpy as jnp
from jax import lax
from jax.experimental import pallas as pl
from jax.experimental.pallas import tpu as pltpu
from jax.sharding import PartitionSpec as P

F32 = jnp.float32
BF16 = jnp.bfloat16


def both_ways(pairs):
    return [(i, j) for i, j in pairs] + [(j, i) for i, j in pairs]


def split(x):
    hi = x.astype(BF16)
    lo = (x - hi.astype(F32)).astype(BF16)
    return hi, lo


def contract(a, b, left):
    return lax.dot_general(a, b, (((left,), (0,)), ((), ())), preferred_element_type=F32)


def dot3(a, b, left=1):
    return contract(a[0], b[0], left) + (contract(a[0], b[1], left) + contract(a[1], b[0], left))


def pack_kernel(par_ref, s_ref, a_ref, e_ref, o_ref, xe_ref, xo_ref):
    m, half = s_ref.shape[0] // 4, e_ref.shape[0] // 2
    py, px = par_ref[0] & 1, par_ref[0] >> 1
    lanes = lax.broadcasted_iota(jnp.int32, (m, 128), 1)
    last = jnp.zeros((m, 128), F32)
    first = jnp.zeros((m, 128), F32)
    for f, ref in enumerate((s_ref, a_ref)):
        for z in range(2):
            rows = [ref[pl.ds(2 * z + y, m, stride=4), :] for y in range(2)]
            here = (pl.ds(f * half, m), pl.ds(z * 128, 128))
            e_ref[here] = jnp.where(py == 0, rows[1], rows[0])
            o_ref[here] = jnp.where(py == 0, rows[0], rows[1])
            for y in range(2):
                j = f * 4 + 2 * z + y
                last = jnp.where(lanes == j, pltpu.roll(rows[y], j + 1, 1), last)
                col = rows[y] if j == 0 else pltpu.roll(rows[y], j, 1)
                first = jnp.where(lanes == j, col, first)
    xe_ref[...] = jnp.where(px == 0, last, first)
    xo_ref[...] = jnp.where(px == 0, first, last)


def interior_kernel(
    par_ref, s_ref, a_ref, xe_ref, xo_ref, up_ref, un_ref, col_ref, relax_ref, wt_ref, dw_ref,
    codes_ref, mask_ref, rs_ref, ra_ref, tab_ref, gain_ref,
):
    m = rs_ref.shape[1]
    low = col_ref.shape[0]
    px = par_ref[0] >> 1
    lanes = lax.broadcasted_iota(jnp.int32, (m, 128), 1)
    xe, xo = xe_ref[...], xo_ref[...]
    xm_all = jnp.where(px == 0, xo, xe)
    xp_all = jnp.where(px == 0, xe, xo)

    def wide(blocks):
        return jnp.concatenate(blocks, axis=1)

    tab_ref[...] = jnp.zeros_like(tab_ref)
    tab_ref[0:1, :] = relax_ref[...]
    tab_ref[1:4, :] = wt_ref[...]
    tab_ref[4:5, :] = dw_ref[...]
    thi, tlo = split(tab_ref[...])
    codes = [codes_ref[q : q + 1, :] for q in range(4)]
    walls = [mask_ref[q : q + 1, :] for q in range(4)]
    sub = lax.broadcasted_iota(jnp.int32, (8, 128), 0)

    def damp_of(row):
        pick = wide([
            jnp.where((sub == 0) | ((sub > 0) & (sub < 4) & (codes[2 * z + row] == sub)), 1.0, 0.0)
            for z in range(2)
        ]).astype(BF16)
        return contract(thi, pick, 0) + contract(tlo, pick, 0)

    def source_of(row):
        pick = wide([jnp.where((sub == 4) & (walls[2 * z + row] != 0), 1.0, 0.0) for z in range(2)]).astype(BF16)
        return contract(thi, pick, 0) + contract(tlo, pick, 0)

    damp = [damp_of(r) for r in range(2)]

    def low_of(ref):
        return wide([ref[pl.ds(2 * z + y, low, stride=4), :] for y in range(2) for z in range(2)])

    s_low, a_low = low_of(s_ref), low_of(a_ref)
    s_low2 = split(s_low)
    adgain = jnp.zeros((low, 512), F32)
    for k in range(low):
        c = col_ref[k]
        u = dot3(split(c + c.T), s_low2)
        adgain = adgain + a_low[k : k + 1, :] * u
        gain_ref[k : k + 1, :] = 0.5 * jnp.sum(s_low * u, axis=0, keepdims=True)
    gain = gain_ref[...]

    pos = [up_ref[d] for d in range(3)]
    neg = [un_ref[d] for d in range(3)]
    pos_x, neg_x = split(pos[0]), split(neg[0])
    pos_y, neg_y = split(pos[1]), split(neg[1])
    diff_z = split(pos[2] - neg[2])

    for f, (ref, out_ref) in enumerate(((s_ref, rs_ref), (a_ref, ra_ref))):
        blk = [[ref[pl.ds(2 * z + y, m, stride=4), :] for z in range(2)] for y in range(2)]
        behind, ahead = [], []
        for y in range(2):
            bs, hs = [], []
            for z in range(2):
                j = f * 4 + 2 * z + y
                b = blk[y][z]
                xm = xm_all if j == 0 else pltpu.roll(xm_all, 128 - j, 1)
                xp = pltpu.roll(xp_all, 127 - j, 1)
                bs.append(b - jnp.where(lanes == 0, xm, pltpu.roll(b, 1, 1)))
                hs.append(jnp.where(lanes == 127, xp, pltpu.roll(b, 127, 1)) - b)
            behind.append(split(wide(bs)))
            ahead.append(split(wide(hs)))
        step_y = split(wide([blk[1][z] - blk[0][z] for z in range(2)]))
        step_z = split(wide([blk[y][0] - blk[y][1] for y in range(2)]))
        if f == 0:
            zpart = dot3(diff_z, step_z)
            rows = [
                dot3(pos_x, behind[0]) + dot3(neg_x, ahead[0]) + dot3(neg_y, step_y),
                dot3(pos_x, behind[1]) + dot3(neg_x, ahead[1]) + dot3(pos_y, step_y),
            ]
        else:
            zpart = dot3(diff_z, step_z, 0)
            rows = [
                -(dot3(pos_x, ahead[0], 0) + dot3(neg_x, behind[0], 0) + dot3(pos_y, step_y, 0)),
                -(dot3(pos_x, ahead[1], 0) + dot3(neg_x, behind[1], 0) + dot3(neg_y, step_y, 0)),
            ]
        for y in range(2):
            zrow = zpart[:, y * 128 : (y + 1) * 128]
            res = rows[y] + wide([zrow, -zrow]) + damp[y] * wide(blk[y])
            if f == 1:
                res = res - source_of(y)
            out_ref[y] = res
            g = gain if f == 0 else adgain
            out_ref[y, 0:low, :] = out_ref[y, 0:low, :] - g[:, y * 256 : (y + 1) * 256]


def finish_row(row, own_ref, recv_ref, rs_ref, ra_ref, up_ref, un_ref, b_ref):
    m, half = rs_ref.shape[1], own_ref.shape[0] // 2
    sign = jnp.where(row == 1, 1.0, -1.0).astype(F32)
    own_s, own_a = own_ref[0:m, :], own_ref[half : half + m, :]
    pos, neg = up_ref[0], un_ref[0]
    with_s = split(jnp.where(row == 1, neg, pos))
    with_a = split(jnp.where(row == 1, pos, neg))
    inverse = split(b_ref[...])
    res_s = rs_ref[0] + dot3(with_s, split(sign * (recv_ref[0:m, :] - own_s)))
    new_s = own_s - 0.5 * dot3(inverse, split(res_s))
    res_a = ra_ref[0] + dot3(with_a, split(sign * (own_a - recv_ref[half : half + m, :])), 0)
    new_a = own_a - 0.5 * dot3(inverse, split(res_a), 0)
    return new_s, new_a


def first_kernel(row_ref, own_ref, recv_ref, rs_ref, ra_ref, up_ref, un_ref, b_ref, out_ref):
    out_ref[0], out_ref[1] = finish_row(row_ref[0], own_ref, recv_ref, rs_ref, ra_ref, up_ref, un_ref, b_ref)


def last_kernel(row_ref, own_ref, recv_ref, rs_ref, ra_ref, up_ref, un_ref, b_ref, done_ref, s_ref, a_ref):
    m = rs_ref.shape[1]
    new = finish_row(row_ref[0], own_ref, recv_ref, rs_ref, ra_ref, up_ref, un_ref, b_ref)
    for f, ref in enumerate((s_ref, a_ref)):
        for z in range(2):
            here = new[f][:, z * 128 : (z + 1) * 128]
            there = done_ref[f, :, z * 128 : (z + 1) * 128]
            ref[pl.ds(2 * z, m, stride=4), :] = jnp.where(row_ref[0] == 0, here, there)
            ref[pl.ds(2 * z + 1, m, stride=4), :] = jnp.where(row_ref[0] == 0, there, here)


def whole(shape):
    return pl.BlockSpec(shape, lambda *_: (0,) * len(shape))


def at_row(shape, index):
    return pl.BlockSpec((1,) + shape[1:], lambda i, row: (row[0] if index is None else index,) + (0,) * (len(shape) - 1))


PARAMS = pltpu.CompilerParams(vmem_limit_bytes=40 * 1024 * 1024)


def call(kernel, name, scalars, args, in_specs, outs, scratch=()):
    flat = jax.tree.leaves(outs)
    return pl.pallas_call(
        kernel,
        name=name,
        out_shape=outs,
        grid_spec=pltpu.PrefetchScalarGridSpec(
            num_scalar_prefetch=1,
            grid=(1,),
            in_specs=in_specs,
            out_specs=jax.tree.map(lambda o: whole(o.shape), outs),
            scratch_shapes=list(scratch),
        ),
        compiler_params=PARAMS,
    )(scalars, *args)


def on_device(
    state, adjoint, upwind_pos, upwind_neg, collision, relax, wall_table, drag_weights, block_inverse,
    cell_codes, wall_mask,
):
    m = state.shape[0]
    low = collision.shape[0]
    gy, gx = lax.axis_index("gy"), lax.axis_index("gx")
    ny, nx = lax.axis_size("gy"), lax.axis_size("gx")
    py, px = gy & 1, gx & 1
    par = (py + 2 * px).astype(jnp.int32).reshape(1)
    s = state.reshape(m * 4, 128)
    a = adjoint.reshape(m * 4, 128)
    rowbuf = jax.ShapeDtypeStruct((2, m, 256), F32)
    swapbuf = jax.ShapeDtypeStruct((2 * ((m + 7) // 8 * 8), 256), F32)
    colbuf = jax.ShapeDtypeStruct((m, 128), F32)
    own_e, own_o, send_xe, send_xo = call(
        pack_kernel, "pack", par, (s, a), [whole(s.shape)] * 2, (swapbuf, swapbuf, colbuf, colbuf)
    )
    even = lambda n: both_ways([(i, i + 1) for i in range(0, n - 1, 2)])
    odd = lambda n: both_ways([(i, i + 1) for i in range(1, n - 1, 2)])
    recv_o = lax.ppermute(own_o, "gy", odd(ny))
    recv_e = lax.ppermute(own_e, "gy", even(ny))
    recv_xe = lax.ppermute(send_xe, "gx", even(nx))
    recv_xo = lax.ppermute(send_xo, "gx", odd(nx))
    interior_args = (
        s, a, recv_xe, recv_xo, upwind_pos, upwind_neg, collision, relax.reshape(1, m), wall_table,
        drag_weights.reshape(1, m), cell_codes.reshape(4, 128), wall_mask.reshape(4, 128),
    )
    res_s, res_a = call(
        interior_kernel, "interior", par, interior_args, [whole(x.shape) for x in interior_args],
        (rowbuf, rowbuf),
        (pltpu.VMEM((8, m), F32), pltpu.VMEM((low, 512), F32)),
    )
    wshape = upwind_pos.shape
    row_specs = [
        whole(swapbuf.shape), whole(swapbuf.shape), at_row(rowbuf.shape, None), at_row(rowbuf.shape, None),
        at_row(wshape, 1), at_row(wshape, 1), whole(block_inverse.shape),
    ]
    tail = (res_s, res_a, upwind_pos, upwind_neg, block_inverse)
    row_e = (1 - py).astype(jnp.int32).reshape(1)
    row_o = py.astype(jnp.int32).reshape(1)
    done = call(first_kernel, "first", row_e, (own_e, recv_e) + tail, row_specs, rowbuf)
    out = jax.ShapeDtypeStruct(s.shape, F32)
    s_next, a_next = call(
        last_kernel, "last", row_o, (own_o, recv_o) + tail + (done,), row_specs + [whole(rowbuf.shape)], (out, out)
    )
    return s_next.reshape(state.shape), a_next.reshape(adjoint.shape)


def solution(mesh):
    field, cells = P(None, None, "gy", "gx"), P(None, "gy", "gx")
    in_specs = (field, field, P(), P(), P(), P(), P(), P(), P(), cells, cells)
    return jax.shard_map(
        on_device, mesh=mesh, in_specs=in_specs, out_specs=(field, field), check_vma=False
    )
```

```python
import jax
import jax.numpy as jnp
from jax import lax
from jax.experimental import pallas as pl
from jax.experimental.pallas import tpu as pltpu
from jax.sharding import PartitionSpec as P


F32 = jnp.float32
BF16 = jnp.bfloat16
DIRECT = 400


def both_ways(pairs):
    return [(i, j) for i, j in pairs] + [(j, i) for i, j in pairs]


def split(x):
    hi = x.astype(BF16)
    lo = (x - hi.astype(F32)).astype(BF16)
    return hi, lo


def dot(a, b):
    return lax.dot_general(a, b, (((1,), (0,)), ((), ())), preferred_element_type=F32)


def up16(n):
    return (n + 15) // 16 * 16


def dot3(left, b, m):
    high = up16(m)
    both = dot(left, b[0])
    return both[0:m, :] + (both[high : high + m, :] + dot(left[0:m, :], b[1]))


def fetch(pairs, sems):
    copies = [pltpu.make_async_copy(src, dst, sems.at[i]) for i, (src, dst) in enumerate(pairs)]
    for c in copies:
        c.start()
    return copies


def block(ref, z, y):
    return ref[pl.ds(2 * z + y, ref.shape[0] // 4, stride=4), :]


def pack_kernel(par_ref, s_hbm, a_hbm, e_ref, n_ref, w_ref, x_ref, s_ref, a_ref, sems):
    m, half = s_ref.shape[0] // 4, e_ref.shape[0] // 2
    direct = n_ref.shape[0]
    py = par_ref[0] & 1
    copies = fetch([(s_hbm, s_ref), (a_hbm, a_ref)], sems)
    lanes = lax.broadcasted_iota(jnp.int32, (m, 128), 1)
    ends = jnp.zeros((m, 128), F32)
    for f, ref in enumerate((s_ref, a_ref)):
        copies[f].wait()
        for z in range(2):
            cells = pl.ds(z * 128, 128)
            rows = [block(ref, z, y) for y in range(2)]
            e_ref[pl.ds(f * half, m), cells] = jnp.where(py == 0, rows[1], rows[0])
            other = jnp.where(py == 0, rows[0], rows[1])
            near = min(m, direct - f * half)
            n_ref[pl.ds(f * half, near), cells] = other[0:near]
            if near < m:
                w_ref[0 : m - near, cells] = other[near:]
            for y in range(2):
                j = f * 4 + 2 * z + y
                ends = jnp.where((lanes >> 1) == j, pltpu.roll(rows[y], 2 * j + 1, 1), ends)
    x_ref[...] = ends


def interior_kernel(
    par_ref, s_hbm, a_hbm, up_hbm, un_hbm, b_hbm, col_hbm, relax_ref, wt_hbm, dw_ref, codes_hbm, mask_hbm, xe_ref,
    rs_ref, ra_ref, wy_ref, wx_ref, binv_ref,
    s_ref, a_ref, up_ref, un_ref, b_ref, col_ref, wt_ref, codes_ref, mask_ref,
    tab_ref, gain_ref, left_ref, lrem_ref, rrem_ref, lcol_ref, u_ref, sems,
):
    m = rs_ref.shape[1]
    high = up16(m)
    low = col_ref.shape[0]
    step = (low + 7) // 8 * 8
    px = (par_ref[0] >> 1) & 1
    copies = fetch(
        [(s_hbm, s_ref), (a_hbm, a_ref), (col_hbm, col_ref), (codes_hbm, codes_ref), (mask_hbm, mask_ref),
         (wt_hbm, wt_ref), (up_hbm, up_ref), (un_hbm, un_ref), (b_hbm, b_ref)],
        sems,
    )
    lanes = lax.broadcasted_iota(jnp.int32, (m, 128), 1)

    def wide(blocks):
        return jnp.concatenate(blocks, axis=1)

    tab_ref[...] = jnp.zeros_like(tab_ref)
    lrem_ref[...] = jnp.zeros_like(lrem_ref)
    rrem_ref[...] = jnp.zeros_like(rrem_ref)
    for c in copies:
        c.wait()

    tab_ref[0, :] = relax_ref[...]
    tab_ref[1:4, :] = wt_ref[...]
    tab_ref[4, :] = dw_ref[...]
    table = tab_ref[...].T
    thi, tlo = split(table)
    sub = lax.broadcasted_iota(jnp.int32, (8, 128), 0)

    def picked(where_row):
        pick = wide([jnp.where(w, 1.0, 0.0) for w in where_row]).astype(BF16)
        return dot(thi, pick) + dot(tlo, pick)

    def damp_of(y):
        codes = [codes_ref[2 * z + y : 2 * z + y + 1, :] for z in range(2)]
        return picked([(sub == 0) | ((sub > 0) & (sub < 4) & (c == sub)) for c in codes])

    def source_of(y):
        walls = [mask_ref[2 * z + y : 2 * z + y + 1, :] for z in range(2)]
        return picked([(sub == 4) & (w != 0) for w in walls])

    def low_of(ref):
        return wide([ref[pl.ds(2 * z + y, low, stride=4), :] for y in range(2) for z in range(2)])

    s_low, a_low = low_of(s_ref), low_of(a_ref)
    s_hi = s_low.astype(BF16).astype(F32)
    s_lo = (s_low - s_hi).astype(BF16).astype(F32)
    gap = jnp.zeros((step - low, 512), F32)
    right = jnp.concatenate([s_hi, gap, s_lo, gap, s_hi, gap, jnp.zeros((128 - 3 * step, 512), F32)], axis=0).astype(BF16)
    lcol_ref[...] = jnp.zeros_like(lcol_ref)
    for k in range(low):
        c = col_ref[k]
        c = c + c.T
        c_hi = c.astype(BF16).astype(F32)
        at = pl.ds(k * step, low)
        lcol_ref[at, 0:low] = c_hi
        lcol_ref[at, step : step + low] = c_hi
        lcol_ref[at, 2 * step : 2 * step + low] = (c - c_hi).astype(BF16).astype(F32)
    u_ref[...] = dot(lcol_ref[...].astype(BF16), right)
    adgain = jnp.zeros((low, 512), F32)
    for k in range(low):
        u = u_ref[pl.ds(k * step, low), :]
        adgain = adgain + a_low[k : k + 1, :] * u
        gain_ref[k : k + 1, :] = 0.5 * jnp.sum(s_low * u, axis=0, keepdims=True)
    gain = gain_ref[...]

    inverse = b_ref[...]
    for f in range(2):
        mats = [up_ref[0], un_ref[0], up_ref[2] - un_ref[2], up_ref[1], un_ref[1]]
        if f == 1:
            mats = [x.T for x in mats]
        for i, x in enumerate(mats):
            hi, lo = split(x)
            left_ref[5 * f + i, 0:m, :] = hi
            left_ref[5 * f + i, high : high + m, :] = lo
            lrem_ref[2 * f, 0:m, 32 * i : 32 * i + m - 256] = hi[:, 256:].astype(F32)
            lrem_ref[2 * f, high : high + m, 32 * i : 32 * i + m - 256] = lo[:, 256:].astype(F32)
        hi, lo = split(inverse if f == 0 else inverse.T)
        binv_ref[f, 0:m, :] = hi
        binv_ref[f, high : high + m, :] = lo
        wy_ref[2 * f] = left_ref[5 * f + (3 if f == 0 else 4)]
        wy_ref[2 * f + 1] = left_ref[5 * f + (4 if f == 0 else 3)]
        wx_ref[f] = jnp.where(px == 0, left_ref[5 * f + f], left_ref[5 * f + 1 - f])

    ends = xe_ref[...]
    ends = jnp.where(px == 0, ends, pltpu.roll(ends, 2, 1))
    for f, (ref, out_ref) in enumerate(((s_ref, rs_ref), (a_ref, ra_ref))):
        sign = 1.0 if f == 0 else -1.0
        blk = [[block(ref, z, y) for z in range(2)] for y in range(2)]
        step_y = wide([sign * (blk[1][z] - blk[0][z]) for z in range(2)])
        for y in range(2):
            bs, hs = [], []
            for z in range(2):
                j = f * 4 + 2 * z + y
                b = blk[y][z]
                end = pltpu.roll(ends, 126 - 2 * j, 1)
                xm = jnp.where(lanes == 0, jnp.where(px == 1, end, 0.0), pltpu.roll(b, 1, 1))
                xp = jnp.where(lanes == 127, jnp.where(px == 0, end, 0.0), pltpu.roll(b, 127, 1))
                bs.append(sign * (b - xm))
                hs.append(sign * (xp - b))
            behind, ahead = wide(bs), wide(hs)
            dz = blk[y][0] - blk[y][1]
            rights = [behind if f == 0 else ahead, ahead if f == 0 else behind, wide([dz, -dz]), step_y]
            use = 4 if (y == 0) == (f == 0) else 3
            total = None
            for i, r in enumerate(rights):
                k = use if i == 3 else i
                part = dot3(left_ref[5 * f + k, :, 0:256], split(r[0:256]), m)
                total = part if total is None else total + part
                rrem_ref[32 * k : 32 * k + m - 256, :] = r[256:m]
            if use == 4:
                rrem_ref[32 * 3 : 32 * 4, :] = jnp.zeros((32, 256), F32)
            else:
                rrem_ref[32 * 4 : 32 * 5, :] = jnp.zeros((32, 256), F32)
            total = total + dot3(lrem_ref[2 * f].astype(BF16), split(rrem_ref[...]), m)
            res = total + damp_of(y) * wide(blk[y])
            if f == 1:
                res = res - source_of(y)
            out_ref[y] = res
            g = gain if f == 0 else adgain
            out_ref[y, 0:low, :] = out_ref[y, 0:low, :] - g[:, y * 256 : (y + 1) * 256]


def finish(row, own, recv, res, wy_ref, binv_ref):
    m = own[0].shape[0]
    sign = jnp.where(row == 1, 1.0, -1.0).astype(F32)
    new = []
    for f in range(2):
        gap = (recv[f] - own[f]) * (sign if f == 0 else -sign)
        total = res[f] + dot3(wy_ref[2 * f + row], split(gap), m)
        new.append(own[f] - 0.5 * dot3(binv_ref[f], split(total), m))
    return new


def first_kernel(par_ref, own_ref, recv_ref, xo_ref, rs_ref, ra_ref, wy_ref, wx_ref, binv_ref, out_ref, res_ref):
    m, half = rs_ref.shape[1], own_ref.shape[0] // 2
    high = up16(m)
    py, px = par_ref[0] & 1, (par_ref[0] >> 1) & 1
    row = 1 - py
    hi, lo = split(xo_ref[...])
    cols = (hi.astype(F32) + pltpu.roll(lo.astype(F32), 16, 1)).astype(BF16)
    lanes = lax.broadcasted_iota(jnp.int32, (m, 128), 1)
    edge = lanes == jnp.where(px == 0, 0, 127)
    res = []
    for f in range(2):
        both = dot(wx_ref[f], cols)
        fix = both[0:m] + (pltpu.roll(both[0:m], 112, 1) + both[high : high + m])
        fix = jnp.where(px == 0, pltpu.roll(fix, 2, 1), fix) * jnp.where((px == 0) == (f == 0), -1.0, 1.0).astype(F32)
        ref = rs_ref if f == 0 else ra_ref
        parts = []
        for r in range(2):
            at = row if r == 0 else py
            per_z = []
            for z in range(2):
                j0 = f * 4 + 2 * z
                fixes = [pltpu.roll(fix, 126 - 2 * (j0 + y), 1) for y in range(2)]
                add = jnp.where(edge, jnp.where(at == 0, fixes[0], fixes[1]), 0.0)
                per_z.append(ref[at, :, z * 128 : (z + 1) * 128] + add)
            parts.append(jnp.concatenate(per_z, axis=1))
        res.append(parts[0])
        res_ref[f] = parts[1]
    own = [own_ref[0:m, :], own_ref[half : half + m, :]]
    recv = [recv_ref[0:m, :], recv_ref[half : half + m, :]]
    new = finish(row, own, recv, res, wy_ref, binv_ref)
    out_ref[0], out_ref[1] = new


def last_kernel(
    par_ref, n_ref, w_ref, recv_n_ref, recv_w_ref, recv_z_ref, res_ref, wy_ref, binv_ref, done_ref, s_ref, a_ref,
    own_ref, recv_ref,
):
    m, half = res_ref.shape[1], own_ref.shape[0] // 2
    row, outer = par_ref[0] & 1, par_ref[0] >> 2
    direct = n_ref.shape[0]
    own_ref[0:direct, :] = n_ref[...]
    own_ref[direct:, :] = w_ref[...]
    recv_ref[0:direct, :] = recv_n_ref[...]
    recv_ref[direct:, :] = jnp.where(outer == 1, recv_z_ref[...], recv_w_ref[...])
    own = [own_ref[0:m, :], own_ref[half : half + m, :]]
    recv = [recv_ref[0:m, :], recv_ref[half : half + m, :]]
    new = finish(row, own, recv, [res_ref[0], res_ref[1]], wy_ref, binv_ref)
    for f, ref in enumerate((s_ref, a_ref)):
        for z in range(2):
            here = new[f][:, z * 128 : (z + 1) * 128]
            there = done_ref[f, :, z * 128 : (z + 1) * 128]
            ref[pl.ds(2 * z, m, stride=4), :] = jnp.where(row == 0, here, there)
            ref[pl.ds(2 * z + 1, m, stride=4), :] = jnp.where(row == 0, there, here)


def whole(shape):
    return pl.BlockSpec(shape, lambda *_: (0,) * len(shape))


IN_HBM = pl.BlockSpec(memory_space=pltpu.HBM)


def call(kernel, scalars, args, outs, scratch=(), hbm=(), us=1.0):
    in_specs = [IN_HBM if i in hbm else whole(x.shape) for i, x in enumerate(args)]
    args = [pltpu.with_memory_space_constraint(x, pltpu.HBM) if i in hbm else x for i, x in enumerate(args)]
    return pl.pallas_call(
        kernel,
        out_shape=outs,
        grid_spec=pltpu.PrefetchScalarGridSpec(
            num_scalar_prefetch=1,
            grid=(1,),
            in_specs=in_specs,
            out_specs=jax.tree.map(lambda o: whole(o.shape), outs),
            scratch_shapes=list(scratch),
        ),
        compiler_params=pltpu.CompilerParams(vmem_limit_bytes=36 * 1024 * 1024),
        cost_estimate=pl.CostEstimate(flops=int(us * 5e8), bytes_accessed=int(us * 1e6), transcendentals=0),
    )(scalars, *args)


def on_device(
    state, adjoint, upwind_pos, upwind_neg, collision, relax, wall_table, drag_weights, block_inverse,
    cell_codes, wall_mask,
):
    m, low = state.shape[0], collision.shape[0]
    half = (m + 7) // 8 * 8
    high, step = up16(m), half // 8 * 0 + (low + 7) // 8 * 8
    gy, gx = lax.axis_index("gy"), lax.axis_index("gx")
    ny, nx = lax.axis_size("gy"), lax.axis_size("gx")
    px = gx & 1
    spot = gy & 3
    outer = 1 - ((spot ^ (spot >> 1)) & 1)
    par = ((gy & 1) + 2 * px + 4 * outer).astype(jnp.int32).reshape(1)
    s = state.reshape(m * 4, 128)
    a = adjoint.reshape(m * 4, 128)
    sds = jax.ShapeDtypeStruct
    rowbuf = sds((2, m, 256), F32)
    relayed = 2 * half - DIRECT
    own_e, own_n, own_w, ends = call(
        pack_kernel, par, (s, a),
        (sds((2 * half, 256), F32), sds((DIRECT, 256), F32), sds((relayed, 256), F32), sds((m, 128), F32)),
        (pltpu.VMEM(s.shape, F32), pltpu.VMEM(s.shape, F32), pltpu.SemaphoreType.DMA((2,))),
        hbm=(0, 1),
    )
    even = lambda n: both_ways([(i, i + 1) for i in range(0, n - 1, 2)])
    odd = lambda n: both_ways([(i, i + 1) for i in range(1, n - 1, 2)])
    quads = range(0, ny, 4)
    around = both_ways([(q, q + 3) for q in quads] + [(q + 1, q + 2) for q in quads])
    onward = [(q, q + 4) for q in quads if q + 4 < ny] + [(q + 7, q + 3) for q in quads if q + 4 < ny]
    recv_n = lax.ppermute(own_n, "gy", odd(ny))
    recv_w = lax.ppermute(own_w, "gy", around)
    recv_e = lax.ppermute(own_e, "gy", even(ny))
    recv_xe = lax.ppermute(ends, "gx", even(nx))
    recv_xo = lax.ppermute(ends, "gx", odd(nx))
    recv_z = lax.ppermute(recv_w, "gy", onward)
    args = (
        s, a, upwind_pos, upwind_neg, block_inverse, collision, relax, wall_table,
        drag_weights, cell_codes.reshape(4, 128), wall_mask.reshape(4, 128), recv_xe,
    )
    hbm = (0, 1, 2, 3, 4, 5, 7, 9, 10)
    weights = lambda n: sds((n, 2 * high, m), BF16)
    res_s, res_a, wy, wx, binv = call(
        interior_kernel, par, args,
        (rowbuf, rowbuf, weights(4), weights(2), weights(2)),
        tuple(pltpu.VMEM(args[i].shape, args[i].dtype) for i in hbm)
        + (
            pltpu.VMEM((8, m), F32), pltpu.VMEM((low, 512), F32), pltpu.VMEM((10, 2 * high, m), BF16),
            pltpu.VMEM((3, 2 * high, 160), F32), pltpu.VMEM((160, 256), F32), pltpu.VMEM((low * step, 128), F32),
            pltpu.VMEM((low * step, 512), F32), pltpu.SemaphoreType.DMA((9,)),
        ),
        hbm=hbm, us=5.0,
    )
    done, res_o = call(first_kernel, par, (own_e, recv_e, recv_xo, res_s, res_a, wy, wx, binv), (rowbuf, rowbuf))
    out = sds(s.shape, F32)
    s_next, a_next = call(
        last_kernel, par,
        (own_n, own_w, recv_n, recv_w, recv_z, res_o, wy, binv, done), (out, out),
        (pltpu.VMEM((2 * half, 256), F32), pltpu.VMEM((2 * half, 256), F32)),
    )
    return s_next.reshape(state.shape), a_next.reshape(adjoint.shape)


def solution(mesh):
    field, cells = P(None, None, "gy", "gx"), P(None, "gy", "gx")
    in_specs = (field, field, P(), P(), P(), P(), P(), P(), P(), cells, cells)
    return jax.shard_map(
        on_device, mesh=mesh, in_specs=in_specs, out_specs=(field, field), check_vma=False
    )
```

```python
import jax
import jax.numpy as jnp
from jax import lax
from jax.experimental import pallas as pl
from jax.experimental.pallas import tpu as pltpu
from jax.sharding import PartitionSpec as P


F32 = jnp.float32
BF16 = jnp.bfloat16
DIRECT = 376


def both_ways(pairs):
    return [(i, j) for i, j in pairs] + [(j, i) for i, j in pairs]


def split(x):
    hi = x.astype(BF16)
    lo = (x - hi.astype(F32)).astype(BF16)
    return hi, lo


def dot(a, b):
    return lax.dot_general(a, b, (((1,), (0,)), ((), ())), preferred_element_type=F32)


def up16(n):
    return (n + 15) // 16 * 16


def dot3(left, b, m):
    high = up16(m)
    both = dot(left, b[0])
    return both[0:m, :] + (both[high : high + m, :] + dot(left[0:m, :], b[1]))


def fetch(pairs, sems):
    copies = [pltpu.make_async_copy(src, dst, sems.at[i]) for i, (src, dst) in enumerate(pairs)]
    for c in copies:
        c.start()
    return copies


def block(ref, z, y):
    return ref[pl.ds(2 * z + y, ref.shape[0] // 4, stride=4), :]


def pack_kernel(par_ref, s_hbm, a_hbm, e_ref, n_ref, w_ref, x_ref, s_ref, a_ref, sems):
    m, half = s_ref.shape[0] // 4, e_ref.shape[0] // 2
    direct = n_ref.shape[0]
    py = par_ref[0] & 1
    copies = fetch([(s_hbm, s_ref), (a_hbm, a_ref)], sems)
    lanes = lax.broadcasted_iota(jnp.int32, (m, 128), 1)
    ends = jnp.zeros((m, 128), F32)
    for f, ref in enumerate((s_ref, a_ref)):
        copies[f].wait()
        for z in range(2):
            cells = pl.ds(z * 128, 128)
            rows = [block(ref, z, y) for y in range(2)]
            e_ref[pl.ds(f * half, m), cells] = jnp.where(py == 0, rows[1], rows[0])
            other = jnp.where(py == 0, rows[0], rows[1])
            near = min(m, direct - f * half)
            n_ref[pl.ds(f * half, near), cells] = other[0:near]
            if near < m:
                w_ref[0 : m - near, cells] = other[near:]
            for y in range(2):
                j = f * 4 + 2 * z + y
                ends = jnp.where((lanes >> 1) == j, pltpu.roll(rows[y], 2 * j + 1, 1), ends)
    x_ref[...] = ends


def merge_kernel(par_ref, own_ref, other_ref, out_ref):
    out_ref[...] = own_ref[...] + pltpu.roll(other_ref[...], 16, 1)


def interior_kernel(
    par_ref, s_hbm, a_hbm, up_hbm, un_hbm, b_hbm, col_hbm, relax_ref, wt_hbm, dw_ref, codes_hbm, mask_hbm, xe_ref,
    rs_ref, ra_ref, wy_ref, wx_ref, binv_ref,
    s_ref, a_ref, up_ref, un_ref, b_ref, col_ref, wt_ref, codes_ref, mask_ref,
    tab_ref, gain_ref, left_ref, lrem_ref, rrem_ref, lcol_ref, u_ref, sems,
):
    m = rs_ref.shape[1]
    high = up16(m)
    low = col_ref.shape[0]
    step = (low + 7) // 8 * 8
    px = (par_ref[0] >> 1) & 1
    copies = fetch(
        [(s_hbm, s_ref), (a_hbm, a_ref), (col_hbm, col_ref), (codes_hbm, codes_ref), (mask_hbm, mask_ref),
         (wt_hbm, wt_ref), (up_hbm, up_ref), (un_hbm, un_ref), (b_hbm, b_ref)],
        sems,
    )
    lanes = lax.broadcasted_iota(jnp.int32, (m, 128), 1)

    def wide(blocks):
        return jnp.concatenate(blocks, axis=1)

    tab_ref[...] = jnp.zeros_like(tab_ref)
    lrem_ref[...] = jnp.zeros_like(lrem_ref)
    rrem_ref[...] = jnp.zeros_like(rrem_ref)
    for c in copies:
        c.wait()

    tab_ref[0, :] = relax_ref[...]
    tab_ref[1:4, :] = wt_ref[...]
    tab_ref[4, :] = dw_ref[...]
    table = tab_ref[...].T
    thi, tlo = split(table)
    sub = lax.broadcasted_iota(jnp.int32, (8, 128), 0)

    def picked(where_row):
        pick = wide([jnp.where(w, 1.0, 0.0) for w in where_row]).astype(BF16)
        return dot(thi, pick) + dot(tlo, pick)

    def damp_of(y):
        codes = [codes_ref[2 * z + y : 2 * z + y + 1, :] for z in range(2)]
        return picked([(sub == 0) | ((sub > 0) & (sub < 4) & (c == sub)) for c in codes])

    def source_of(y):
        walls = [mask_ref[2 * z + y : 2 * z + y + 1, :] for z in range(2)]
        return picked([(sub == 4) & (w != 0) for w in walls])

    def low_of(ref):
        return wide([ref[pl.ds(2 * z + y, low, stride=4), :] for y in range(2) for z in range(2)])

    s_low, a_low = low_of(s_ref), low_of(a_ref)
    s_hi = s_low.astype(BF16).astype(F32)
    s_lo = (s_low - s_hi).astype(BF16).astype(F32)
    gap = jnp.zeros((step - low, 512), F32)
    right = jnp.concatenate([s_hi, gap, s_lo, gap, s_hi, gap, jnp.zeros((128 - 3 * step, 512), F32)], axis=0).astype(BF16)
    lcol_ref[...] = jnp.zeros_like(lcol_ref)
    for k in range(low):
        c = col_ref[k]
        c = c + c.T
        c_hi = c.astype(BF16).astype(F32)
        at = pl.ds(k * step, low)
        lcol_ref[at, 0:low] = c_hi
        lcol_ref[at, step : step + low] = c_hi
        lcol_ref[at, 2 * step : 2 * step + low] = (c - c_hi).astype(BF16).astype(F32)
    u_ref[...] = dot(lcol_ref[...].astype(BF16), right)
    adgain = jnp.zeros((low, 512), F32)
    for k in range(low):
        u = u_ref[pl.ds(k * step, low), :]
        adgain = adgain + a_low[k : k + 1, :] * u
        gain_ref[k : k + 1, :] = 0.5 * jnp.sum(s_low * u, axis=0, keepdims=True)
    gain = gain_ref[...]

    inverse = b_ref[...]
    for f in range(2):
        mats = [up_ref[0], un_ref[0], up_ref[2] - un_ref[2], up_ref[1], un_ref[1]]
        if f == 1:
            mats = [x.T for x in mats]
        for i, x in enumerate(mats):
            hi, lo = split(x)
            left_ref[5 * f + i, 0:m, :] = hi
            left_ref[5 * f + i, high : high + m, :] = lo
            lrem_ref[2 * f, 0:m, 32 * i : 32 * i + m - 256] = hi[:, 256:].astype(F32)
            lrem_ref[2 * f, high : high + m, 32 * i : 32 * i + m - 256] = lo[:, 256:].astype(F32)
        hi, lo = split(inverse if f == 0 else inverse.T)
        binv_ref[f, 0:m, :] = hi
        binv_ref[f, high : high + m, :] = lo
        wy_ref[2 * f] = left_ref[5 * f + (3 if f == 0 else 4)]
        wy_ref[2 * f + 1] = left_ref[5 * f + (4 if f == 0 else 3)]
        wx_ref[f] = jnp.where(px == 0, left_ref[5 * f + f], left_ref[5 * f + 1 - f])

    ends = xe_ref[...]
    ends = jnp.where(px == 0, ends, pltpu.roll(ends, 2, 1))
    for f, (ref, out_ref) in enumerate(((s_ref, rs_ref), (a_ref, ra_ref))):
        sign = 1.0 if f == 0 else -1.0
        blk = [[block(ref, z, y) for z in range(2)] for y in range(2)]
        step_y = wide([sign * (blk[1][z] - blk[0][z]) for z in range(2)])
        for y in range(2):
            bs, hs = [], []
            for z in range(2):
                j = f * 4 + 2 * z + y
                b = blk[y][z]
                end = pltpu.roll(ends, 126 - 2 * j, 1)
                xm = jnp.where(lanes == 0, jnp.where(px == 1, end, 0.0), pltpu.roll(b, 1, 1))
                xp = jnp.where(lanes == 127, jnp.where(px == 0, end, 0.0), pltpu.roll(b, 127, 1))
                bs.append(sign * (b - xm))
                hs.append(sign * (xp - b))
            behind, ahead = wide(bs), wide(hs)
            dz = blk[y][0] - blk[y][1]
            rights = [behind if f == 0 else ahead, ahead if f == 0 else behind, wide([dz, -dz]), step_y]
            use = 4 if (y == 0) == (f == 0) else 3
            total = None
            for i, r in enumerate(rights):
                k = use if i == 3 else i
                part = dot3(left_ref[5 * f + k, :, 0:256], split(r[0:256]), m)
                total = part if total is None else total + part
                rrem_ref[32 * k : 32 * k + m - 256, :] = r[256:m]
            if use == 4:
                rrem_ref[32 * 3 : 32 * 4, :] = jnp.zeros((32, 256), F32)
            else:
                rrem_ref[32 * 4 : 32 * 5, :] = jnp.zeros((32, 256), F32)
            total = total + dot3(lrem_ref[2 * f].astype(BF16), split(rrem_ref[...]), m)
            res = total + damp_of(y) * wide(blk[y])
            if f == 1:
                res = res - source_of(y)
            out_ref[y] = res
            g = gain if f == 0 else adgain
            out_ref[y, 0:low, :] = out_ref[y, 0:low, :] - g[:, y * 256 : (y + 1) * 256]


def finish(row, own, recv, res, wy_ref, binv_ref):
    m = own[0].shape[0]
    sign = jnp.where(row == 1, 1.0, -1.0).astype(F32)
    new = []
    for f in range(2):
        gap = (recv[f] - own[f]) * (sign if f == 0 else -sign)
        total = res[f] + dot3(wy_ref[2 * f + row], split(gap), m)
        new.append(own[f] - 0.5 * dot3(binv_ref[f], split(total), m))
    return new


def first_kernel(par_ref, own_ref, recv_ref, xo_ref, xf_ref, rs_ref, ra_ref, wy_ref, wx_ref, binv_ref, out_ref, res_ref):
    m, half = rs_ref.shape[1], own_ref.shape[0] // 2
    high = up16(m)
    py, px = par_ref[0] & 1, (par_ref[0] >> 1) & 1
    row = 1 - py
    outer = par_ref[0] >> 2
    lanes = lax.broadcasted_iota(jnp.int32, (m, 128), 1)
    came = jnp.where(outer == 1, pltpu.roll(xf_ref[...], 112, 1), xo_ref[...])
    hi, lo = split(jnp.where(lanes < 16, came, 0.0))
    cols = (hi.astype(F32) + pltpu.roll(lo.astype(F32), 16, 1)).astype(BF16)
    edge = lanes == jnp.where(px == 0, 0, 127)
    res = []
    for f in range(2):
        both = dot(wx_ref[f], cols)
        fix = both[0:m] + (pltpu.roll(both[0:m], 112, 1) + both[high : high + m])
        fix = jnp.where(px == 0, pltpu.roll(fix, 2, 1), fix) * jnp.where((px == 0) == (f == 0), -1.0, 1.0).astype(F32)
        ref = rs_ref if f == 0 else ra_ref
        parts = []
        for r in range(2):
            at = row if r == 0 else py
            per_z = []
            for z in range(2):
                j0 = f * 4 + 2 * z
                fixes = [pltpu.roll(fix, 126 - 2 * (j0 + y), 1) for y in range(2)]
                add = jnp.where(edge, jnp.where(at == 0, fixes[0], fixes[1]), 0.0)
                per_z.append(ref[at, :, z * 128 : (z + 1) * 128] + add)
            parts.append(jnp.concatenate(per_z, axis=1))
        res.append(parts[0])
        res_ref[f] = parts[1]
    own = [own_ref[0:m, :], own_ref[half : half + m, :]]
    recv = [recv_ref[0:m, :], recv_ref[half : half + m, :]]
    new = finish(row, own, recv, res, wy_ref, binv_ref)
    out_ref[0], out_ref[1] = new


def last_kernel(
    par_ref, n_ref, w_ref, recv_n_ref, recv_w_ref, recv_z_ref, res_ref, wy_ref, binv_ref, done_ref, s_ref, a_ref,
    own_ref, recv_ref,
):
    m, half = res_ref.shape[1], own_ref.shape[0] // 2
    row, outer = par_ref[0] & 1, par_ref[0] >> 2
    direct = n_ref.shape[0]
    own_ref[0:direct, :] = n_ref[...]
    own_ref[direct:, :] = w_ref[...]
    recv_ref[0:direct, :] = recv_n_ref[...]
    recv_ref[direct:, :] = jnp.where(outer == 1, recv_z_ref[...], recv_w_ref[...])
    own = [own_ref[0:m, :], own_ref[half : half + m, :]]
    recv = [recv_ref[0:m, :], recv_ref[half : half + m, :]]
    new = finish(row, own, recv, [res_ref[0], res_ref[1]], wy_ref, binv_ref)
    for f, ref in enumerate((s_ref, a_ref)):
        for z in range(2):
            here = new[f][:, z * 128 : (z + 1) * 128]
            there = done_ref[f, :, z * 128 : (z + 1) * 128]
            ref[pl.ds(2 * z, m, stride=4), :] = jnp.where(row == 0, here, there)
            ref[pl.ds(2 * z + 1, m, stride=4), :] = jnp.where(row == 0, there, here)


def whole(shape):
    return pl.BlockSpec(shape, lambda *_: (0,) * len(shape))


IN_HBM = pl.BlockSpec(memory_space=pltpu.HBM)


def call(kernel, scalars, args, outs, scratch=(), hbm=(), us=1.0):
    in_specs = [IN_HBM if i in hbm else whole(x.shape) for i, x in enumerate(args)]
    args = [pltpu.with_memory_space_constraint(x, pltpu.HBM) if i in hbm else x for i, x in enumerate(args)]
    return pl.pallas_call(
        kernel,
        out_shape=outs,
        grid_spec=pltpu.PrefetchScalarGridSpec(
            num_scalar_prefetch=1,
            grid=(1,),
            in_specs=in_specs,
            out_specs=jax.tree.map(lambda o: whole(o.shape), outs),
            scratch_shapes=list(scratch),
        ),
        compiler_params=pltpu.CompilerParams(vmem_limit_bytes=36 * 1024 * 1024),
        cost_estimate=pl.CostEstimate(flops=int(us * 5e8), bytes_accessed=int(us * 1e6), transcendentals=0),
    )(scalars, *args)


def on_device(
    state, adjoint, upwind_pos, upwind_neg, collision, relax, wall_table, drag_weights, block_inverse,
    cell_codes, wall_mask,
):
    m, low = state.shape[0], collision.shape[0]
    half = (m + 7) // 8 * 8
    high, step = up16(m), half // 8 * 0 + (low + 7) // 8 * 8
    gy, gx = lax.axis_index("gy"), lax.axis_index("gx")
    ny, nx = lax.axis_size("gy"), lax.axis_size("gx")
    px = gx & 1
    spot = gy & 3
    outer = 1 - ((spot ^ (spot >> 1)) & 1)
    par = ((gy & 1) + 2 * px + 4 * outer).astype(jnp.int32).reshape(1)
    s = state.reshape(m * 4, 128)
    a = adjoint.reshape(m * 4, 128)
    sds = jax.ShapeDtypeStruct
    rowbuf = sds((2, m, 256), F32)
    relayed = 2 * half - DIRECT
    own_e, own_n, own_w, ends = call(
        pack_kernel, par, (s, a),
        (sds((2 * half, 256), F32), sds((DIRECT, 256), F32), sds((relayed, 256), F32), sds((m, 128), F32)),
        (pltpu.VMEM(s.shape, F32), pltpu.VMEM(s.shape, F32), pltpu.SemaphoreType.DMA((2,))),
        hbm=(0, 1),
    )
    even = lambda n: both_ways([(i, i + 1) for i in range(0, n - 1, 2)])
    odd = lambda n: both_ways([(i, i + 1) for i in range(1, n - 1, 2)])
    quads = range(0, ny, 4)
    around = both_ways([(q, q + 3) for q in quads] + [(q + 1, q + 2) for q in quads])
    onward = [(q, q + 4) for q in quads if q + 4 < ny] + [(q + 7, q + 3) for q in quads if q + 4 < ny]
    recv_n = lax.ppermute(own_n, "gy", odd(ny))
    recv_w = lax.ppermute(own_w, "gy", around)
    recv_e = lax.ppermute(own_e, "gy", even(ny))
    recv_xe = lax.ppermute(ends, "gx", even(nx))
    ends_p = lax.ppermute(ends, "gy", even(ny))
    ends_m = call(merge_kernel, par, (ends, ends_p), sds((m, 128), F32))
    inner = [g for g in range(ny) if g % 4 in (1, 2)]
    recv_xo = lax.ppermute(ends_m, ("gx", "gy"), [(i * ny + g, j * ny + g) for i, j in odd(nx) for g in inner])
    recv_xf = lax.ppermute(recv_xo, "gy", even(ny))
    recv_z = lax.ppermute(recv_w, "gy", onward)
    args = (
        s, a, upwind_pos, upwind_neg, block_inverse, collision, relax, wall_table,
        drag_weights, cell_codes.reshape(4, 128), wall_mask.reshape(4, 128), recv_xe,
    )
    hbm = (0, 1, 2, 3, 4, 5, 7, 9, 10)
    weights = lambda n: sds((n, 2 * high, m), BF16)
    res_s, res_a, wy, wx, binv = call(
        interior_kernel, par, args,
        (rowbuf, rowbuf, weights(4), weights(2), weights(2)),
        tuple(pltpu.VMEM(args[i].shape, args[i].dtype) for i in hbm)
        + (
            pltpu.VMEM((8, m), F32), pltpu.VMEM((low, 512), F32), pltpu.VMEM((10, 2 * high, m), BF16),
            pltpu.VMEM((3, 2 * high, 160), F32), pltpu.VMEM((160, 256), F32), pltpu.VMEM((low * step, 128), F32),
            pltpu.VMEM((low * step, 512), F32), pltpu.SemaphoreType.DMA((9,)),
        ),
        hbm=hbm, us=5.0,
    )
    done, res_o = call(
        first_kernel, par, (own_e, recv_e, recv_xo, recv_xf, res_s, res_a, wy, wx, binv), (rowbuf, rowbuf)
    )
    out = sds(s.shape, F32)
    s_next, a_next = call(
        last_kernel, par,
        (own_n, own_w, recv_n, recv_w, recv_z, res_o, wy, binv, done), (out, out),
        (pltpu.VMEM((2 * half, 256), F32), pltpu.VMEM((2 * half, 256), F32)),
    )
    return s_next.reshape(state.shape), a_next.reshape(adjoint.shape)


def solution(mesh):
    field, cells = P(None, None, "gy", "gx"), P(None, "gy", "gx")
    in_specs = (field, field, P(), P(), P(), P(), P(), P(), P(), cells, cells)
    return jax.shard_map(
        on_device, mesh=mesh, in_specs=in_specs, out_specs=(field, field), check_vma=False
    )
```

```python
import jax
import jax.numpy as jnp
from jax import lax
from jax.experimental import pallas as pl
from jax.experimental.pallas import tpu as pltpu
from jax.sharding import PartitionSpec as P


F32 = jnp.float32
BF16 = jnp.bfloat16
DIRECT = 376


def both_ways(pairs):
    return [(i, j) for i, j in pairs] + [(j, i) for i, j in pairs]


def split(x):
    hi = x.astype(BF16)
    lo = (x - hi.astype(F32)).astype(BF16)
    return hi, lo


def dot(a, b):
    return lax.dot_general(a, b, (((1,), (0,)), ((), ())), preferred_element_type=F32)


def up16(n):
    return (n + 15) // 16 * 16


def dot3(left, b, m):
    high = up16(m)
    both = dot(left, b[0])
    return both[0:m, :] + (both[high : high + m, :] + dot(left[0:m, :], b[1]))


def fetch(pairs, sems):
    copies = [pltpu.make_async_copy(src, dst, sems.at[i]) for i, (src, dst) in enumerate(pairs)]
    for c in copies:
        c.start()
    return copies


def block(ref, z, y):
    return ref[pl.ds(2 * z + y, ref.shape[0] // 4, stride=4), :]


def fold(x, rows):
    return sum(pltpu.roll(x[g * rows : (g + 1) * rows], 32 * g, 1) if g else x[0:rows] for g in range(4))


def unfold(x, m):
    groups = [pltpu.roll(x, 128 - 32 * g, 1) if g else x for g in range(4)]
    return jnp.concatenate(groups, axis=0)[0:m]


def pack_kernel(par_ref, s_hbm, a_hbm, e_ref, n_ref, w_ref, x_ref, s_ref, a_ref, sems):
    m, half = s_ref.shape[0] // 4, e_ref.shape[0] // 2
    direct = n_ref.shape[0]
    py = par_ref[0] & 1
    copies = fetch([(s_hbm, s_ref), (a_hbm, a_ref)], sems)
    lanes = lax.broadcasted_iota(jnp.int32, (m, 128), 1)
    ends = jnp.zeros((m, 128), F32)
    for f, ref in enumerate((s_ref, a_ref)):
        copies[f].wait()
        for z in range(2):
            cells = pl.ds(z * 128, 128)
            rows = [block(ref, z, y) for y in range(2)]
            e_ref[pl.ds(f * half, m), cells] = jnp.where(py == 0, rows[1], rows[0])
            other = jnp.where(py == 0, rows[0], rows[1])
            near = min(m, direct - f * half)
            n_ref[pl.ds(f * half, near), cells] = other[0:near]
            if near < m:
                w_ref[0 : m - near, cells] = other[near:]
            for y in range(2):
                j = f * 4 + 2 * z + y
                ends = jnp.where((lanes >> 1) == j, pltpu.roll(rows[y], 2 * j + 1, 1), ends)
    rows = x_ref.shape[0]
    x_ref[...] = fold(jnp.concatenate([ends, jnp.zeros((4 * rows - m, 128), F32)], axis=0), rows)


def merge_kernel(par_ref, own_ref, other_ref, out_ref):
    out_ref[...] = own_ref[...] + pltpu.roll(other_ref[...], 16, 1)


def prep_kernel(
    par_ref, s_hbm, a_hbm, up_ref, un_ref, b_hbm, col_ref,
    s_ref, a_ref, left_ref, lrem_ref, binv_ref, comp_ref, lcol_ref,
    b_ref, rem_ref, cmat_ref, sems,
):
    m = b_ref.shape[0]
    high = up16(m)
    low = col_ref.shape[0]
    step = (low + 7) // 8 * 8
    row = par_ref[0] & 1
    copies = fetch(
        [(b_hbm, b_ref), (s_hbm, s_ref), (a_hbm, a_ref)], sems
    )
    rem_ref[...] = jnp.zeros_like(rem_ref)
    cmat_ref[...] = jnp.zeros_like(cmat_ref)
    meets = []
    for f in range(2):
        mats = [up_ref[0], un_ref[0], up_ref[2] - un_ref[2], up_ref[1], un_ref[1]]
        if f == 1:
            mats = [x.T for x in mats]
        for i, x in enumerate(mats):
            hi, lo = split(x)
            left_ref[5 * f + i, 0:m, :] = hi
            left_ref[5 * f + i, high : high + m, :] = lo
            rem_ref[f, 0:m, 32 * i : 32 * i + m - 256] = hi[:, 256:].astype(F32)
            rem_ref[f, high : high + m, 32 * i : 32 * i + m - 256] = lo[:, 256:].astype(F32)
        lrem_ref[f] = rem_ref[f].astype(BF16)
        meets.append(jnp.where((row == 0) == (f == 0), mats[3], mats[4]))
    copies[0].wait()
    for f in range(2):
        hi, lo = split(b_ref[...] if f == 0 else b_ref[...].T)
        binv_ref[f, 0:m, :] = hi
        binv_ref[f, high : high + m, :] = lo
        scale = jnp.where((row == 1) == (f == 0), -0.5, 0.5).astype(F32)
        hi, lo = split(scale * dot3(binv_ref[f], split(meets[f]), m))
        comp_ref[f, 0:m, :] = hi
        comp_ref[f, high : high + m, :] = lo
    for k in range(low):
        c = col_ref[k]
        c = c + c.T
        c_hi = c.astype(BF16).astype(F32)
        at = pl.ds(k * step, low)
        cmat_ref[at, 0:low] = c_hi
        cmat_ref[at, step : step + low] = c_hi
        cmat_ref[at, 2 * step : 2 * step + low] = (c - c_hi).astype(BF16).astype(F32)
    lcol_ref[...] = cmat_ref[...].astype(BF16)
    copies[1].wait()
    copies[2].wait()


def interior_kernel(
    par_ref, s_ref, a_ref, left_ref, lrem_ref, lcol_ref, relax_ref, wt_hbm, dw_ref, codes_hbm, mask_hbm, xe_ref,
    rs_ref, ra_ref, wt_ref, codes_ref, mask_ref, tab_ref, gain_ref, rrem_ref, u_ref, sems,
):
    m = rs_ref.shape[1]
    low = gain_ref.shape[0]
    step = (low + 7) // 8 * 8
    px = (par_ref[0] >> 1) & 1
    copies = fetch([(codes_hbm, codes_ref), (mask_hbm, mask_ref), (wt_hbm, wt_ref)], sems)
    lanes = lax.broadcasted_iota(jnp.int32, (m, 128), 1)

    def wide(blocks):
        return jnp.concatenate(blocks, axis=1)

    tab_ref[...] = jnp.zeros_like(tab_ref)
    rrem_ref[...] = jnp.zeros_like(rrem_ref)

    def low_of(ref):
        return wide([ref[pl.ds(2 * z + y, low, stride=4), :] for y in range(2) for z in range(2)])

    s_low, a_low = low_of(s_ref), low_of(a_ref)
    s_hi = s_low.astype(BF16).astype(F32)
    s_lo = (s_low - s_hi).astype(BF16).astype(F32)
    gap = jnp.zeros((step - low, 512), F32)
    right = jnp.concatenate([s_hi, gap, s_lo, gap, s_hi, gap, jnp.zeros((128 - 3 * step, 512), F32)], axis=0).astype(BF16)
    u_ref[...] = dot(lcol_ref[...], right)
    adgain = jnp.zeros((low, 512), F32)
    for k in range(low):
        u = u_ref[pl.ds(k * step, low), :]
        adgain = adgain + a_low[k : k + 1, :] * u
        gain_ref[k : k + 1, :] = 0.5 * jnp.sum(s_low * u, axis=0, keepdims=True)
    gain = gain_ref[...]

    for c in copies:
        c.wait()
    tab_ref[0, :] = relax_ref[...]
    tab_ref[1:4, :] = wt_ref[...]
    tab_ref[4, :] = dw_ref[...]
    tab_hi = tab_ref[0:8, :].astype(BF16).astype(F32)
    tab_ref[8:16, :] = tab_ref[0:8, :] - tab_hi
    tab_ref[0:8, :] = tab_hi
    table = tab_ref[...].T.astype(BF16)
    sub = lax.broadcasted_iota(jnp.int32, (16, 128), 0) & 7

    def picked(where_row):
        return dot(table, wide([jnp.where(w, 1.0, 0.0) for w in where_row]).astype(BF16))

    codes = [codes_ref[q : q + 1, :] for q in range(4)]
    walls = [mask_ref[q : q + 1, :] for q in range(4)]
    damp = [
        picked([(sub == 0) | ((sub > 0) & (sub < 4) & (codes[2 * z + y] == sub)) for z in range(2)]) for y in range(2)
    ]
    source = [picked([(sub == 4) & (walls[2 * z + y] != 0) for z in range(2)]) for y in range(2)]

    ends = unfold(xe_ref[...], m)
    ends = jnp.where(px == 0, ends, pltpu.roll(ends, 2, 1))
    for f, (ref, out_ref) in enumerate(((s_ref, rs_ref), (a_ref, ra_ref))):
        sign = 1.0 if f == 0 else -1.0
        blk = [[block(ref, z, y) for z in range(2)] for y in range(2)]
        step_y = wide([sign * (blk[1][z] - blk[0][z]) for z in range(2)])
        for y in range(2):
            bs, hs = [], []
            for z in range(2):
                j = f * 4 + 2 * z + y
                b = blk[y][z]
                end = pltpu.roll(ends, 126 - 2 * j, 1)
                xm = jnp.where(lanes == 0, jnp.where(px == 1, end, 0.0), pltpu.roll(b, 1, 1))
                xp = jnp.where(lanes == 127, jnp.where(px == 0, end, 0.0), pltpu.roll(b, 127, 1))
                bs.append(sign * (b - xm))
                hs.append(sign * (xp - b))
            behind, ahead = wide(bs), wide(hs)
            dz = blk[y][0] - blk[y][1]
            rights = [behind if f == 0 else ahead, ahead if f == 0 else behind, wide([dz, -dz]), step_y]
            use = 4 if (y == 0) == (f == 0) else 3
            total = damp[y] * wide(blk[y])
            if f == 1:
                total = total - source[y]
            for i, r in enumerate(rights):
                k = use if i == 3 else i
                total = total + dot3(left_ref[5 * f + k, :, 0:256], split(r[0:256]), m)
                rrem_ref[32 * k : 32 * k + m - 256, :] = r[256:m]
            idle = 7 - use
            rrem_ref[32 * idle : 32 * idle + 32, :] = jnp.zeros((32, 256), F32)
            out_ref[y] = total + dot3(lrem_ref[f], split(rrem_ref[...]), m)
            g = gain if f == 0 else adgain
            out_ref[y, 0:low, :] = out_ref[y, 0:low, :] - g[:, y * 256 : (y + 1) * 256]


def first_kernel(
    par_ref, own_ref, recv_ref, n_ref, w_ref, xo_ref, xf_ref, rs_ref, ra_ref, left_ref, binv_ref, out_ref, pre_ref,
):
    m, half = rs_ref.shape[1], own_ref.shape[0] // 2
    high = up16(m)
    py, px = par_ref[0] & 1, (par_ref[0] >> 1) & 1
    row = 1 - py
    outer = par_ref[0] >> 2
    lanes = lax.broadcasted_iota(jnp.int32, (m, 128), 1)
    came = jnp.where(outer == 1, pltpu.roll(xf_ref[...], 112, 1), xo_ref[...])
    hi, lo = split(jnp.where(lanes < 16, unfold(came, m), 0.0))
    cols = (hi.astype(F32) + pltpu.roll(lo.astype(F32), 16, 1)).astype(BF16)
    edge = lanes == jnp.where(px == 0, 0, 127)
    near = n_ref.shape[0] - half
    own_o = [n_ref[0:m, :], jnp.concatenate([n_ref[half:, :], w_ref[0 : m - near, :]], axis=0)]
    for f in range(2):
        both = dot(left_ref[5 * f + (px if f == 0 else 1 - px)], cols)
        fix = both[0:m] + (pltpu.roll(both[0:m], 112, 1) + both[high : high + m])
        fix = jnp.where(px == 0, pltpu.roll(fix, 2, 1), fix) * jnp.where((px == 0) == (f == 0), -1.0, 1.0).astype(F32)
        ref = rs_ref if f == 0 else ra_ref
        fixes = [[pltpu.roll(fix, 126 - 2 * (f * 4 + 2 * z + y), 1) for y in range(2)] for z in range(2)]

        def fixed(at):
            return jnp.concatenate(
                [
                    ref[at, :, z * 128 : (z + 1) * 128]
                    + jnp.where(edge, jnp.where(at == 0, fixes[z][0], fixes[z][1]), 0.0)
                    for z in range(2)
                ],
                axis=1,
            )

        own = own_ref[f * half : f * half + m, :]
        gap = recv_ref[f * half : f * half + m, :] - own
        gap = gap * jnp.where((row == 1) == (f == 0), 1.0, -1.0).astype(F32)
        meet = 3 + row if f == 0 else 4 - row
        total = fixed(row) + dot3(left_ref[5 * f + meet], split(gap), m)
        out_ref[f] = own - 0.5 * dot3(binv_ref[f], split(total), m)
        pre_ref[f] = own_o[f] - 0.5 * dot3(binv_ref[f], split(fixed(py)), m)


def last_kernel(
    par_ref, n_ref, w_ref, recv_n_ref, recv_w_ref, recv_z_ref, pre_ref, comp_ref, done_ref, s_hbm, a_hbm,
    s_ref, a_ref, sems,
):
    m, direct = pre_ref.shape[1], n_ref.shape[0]
    half = (m + 7) // 8 * 8
    row, outer = par_ref[0] & 1, par_ref[0] >> 2
    near = direct - half
    copies = [pltpu.make_async_copy(s_ref, s_hbm, sems.at[0]), pltpu.make_async_copy(a_ref, a_hbm, sems.at[1])]
    for f, ref in enumerate((s_ref, a_ref)):
        if f == 0:
            gap = recv_n_ref[0:m, :] - n_ref[0:m, :]
        else:
            relayed = jnp.where(outer == 1, recv_z_ref[...], recv_w_ref[...]) - w_ref[...]
            gap = jnp.concatenate([recv_n_ref[half:, :] - n_ref[half:, :], relayed[0 : m - near]], axis=0)
        new = pre_ref[f] + dot3(comp_ref[f], split(gap), m)
        for z in range(2):
            here = new[:, z * 128 : (z + 1) * 128]
            there = done_ref[f, :, z * 128 : (z + 1) * 128]
            ref[pl.ds(2 * z, m, stride=4), :] = jnp.where(row == 0, here, there)
            ref[pl.ds(2 * z + 1, m, stride=4), :] = jnp.where(row == 0, there, here)
        copies[f].start()
    for c in copies:
        c.wait()


def whole(shape):
    return pl.BlockSpec(shape, lambda *_: (0,) * len(shape))


IN_HBM = pl.BlockSpec(memory_space=pltpu.HBM)


def call(kernel, scalars, args, outs, scratch=(), hbm=(), us=1.0, outs_hbm=False):
    in_specs = [IN_HBM if i in hbm else whole(x.shape) for i, x in enumerate(args)]
    args = [pltpu.with_memory_space_constraint(x, pltpu.HBM) if i in hbm else x for i, x in enumerate(args)]
    return pl.pallas_call(
        kernel,
        out_shape=outs,
        grid_spec=pltpu.PrefetchScalarGridSpec(
            num_scalar_prefetch=1,
            grid=(1,),
            in_specs=in_specs,
            out_specs=jax.tree.map(lambda o: IN_HBM if outs_hbm else whole(o.shape), outs),
            scratch_shapes=list(scratch),
        ),
        compiler_params=pltpu.CompilerParams(vmem_limit_bytes=36 * 1024 * 1024),
        cost_estimate=pl.CostEstimate(flops=int(us * 5e8), bytes_accessed=int(us * 1e6), transcendentals=0),
    )(scalars, *args)


def on_device(
    state, adjoint, upwind_pos, upwind_neg, collision, relax, wall_table, drag_weights, block_inverse,
    cell_codes, wall_mask,
):
    m, low = state.shape[0], collision.shape[0]
    half = (m + 7) // 8 * 8
    high, step = up16(m), (low + 7) // 8 * 8
    gy, gx = lax.axis_index("gy"), lax.axis_index("gx")
    ny, nx = lax.axis_size("gy"), lax.axis_size("gx")
    px = gx & 1
    spot = gy & 3
    outer = 1 - ((spot ^ (spot >> 1)) & 1)
    par = ((gy & 1) + 2 * px + 4 * outer).astype(jnp.int32).reshape(1)
    s = state.reshape(m * 4, 128)
    a = adjoint.reshape(m * 4, 128)
    sds = jax.ShapeDtypeStruct
    rowbuf = sds((2, m, 256), F32)
    colbuf = sds(((m + 31) // 32 * 8, 128), F32)
    relayed = 2 * half - DIRECT
    own_e, own_n, own_w, ends = call(
        pack_kernel, par, (s, a),
        (sds((2 * half, 256), F32), sds((DIRECT, 256), F32), sds((relayed, 256), F32), colbuf),
        (pltpu.VMEM(s.shape, F32), pltpu.VMEM(s.shape, F32), pltpu.SemaphoreType.DMA((2,))),
        hbm=(0, 1),
    )
    even = lambda n: both_ways([(i, i + 1) for i in range(0, n - 1, 2)])
    odd = lambda n: both_ways([(i, i + 1) for i in range(1, n - 1, 2)])
    quads = range(0, ny, 4)
    around = both_ways([(q, q + 3) for q in quads] + [(q + 1, q + 2) for q in quads])
    onward = [(q, q + 4) for q in quads if q + 4 < ny] + [(q + 7, q + 3) for q in quads if q + 4 < ny]
    recv_n = lax.ppermute(own_n, "gy", odd(ny))
    recv_w = lax.ppermute(own_w, "gy", around)
    recv_e = lax.ppermute(own_e, "gy", even(ny))
    recv_xe = lax.ppermute(ends, "gx", even(nx))
    ends_p = lax.ppermute(ends, "gy", even(ny))
    ends_m = call(merge_kernel, par, (ends, ends_p), colbuf)
    inner = [g for g in range(ny) if g % 4 in (1, 2)]
    recv_xo = lax.ppermute(ends_m, ("gx", "gy"), [(i * ny + g, j * ny + g) for i, j in odd(nx) for g in inner])
    recv_xf = lax.ppermute(recv_xo, "gy", even(ny))
    recv_z = lax.ppermute(recv_w, "gy", onward)
    args = (s, a, upwind_pos, upwind_neg, block_inverse, collision)
    weights = lambda n, k: sds((n, 2 * high, k), BF16)
    s_in, a_in, left, lrem, binv, comp, lcol = call(
        prep_kernel, par, args,
        (
            sds(s.shape, F32), sds(a.shape, F32), weights(10, m), weights(2, 160), weights(2, m), weights(2, m),
            sds((low * step, 128), BF16),
        ),
        (
            pltpu.VMEM((m, m), F32), pltpu.VMEM((2, 2 * high, 160), F32), pltpu.VMEM((low * step, 128), F32), pltpu.SemaphoreType.DMA((3,)),
        ),
        hbm=(0, 1, 4), us=3.0,
    )
    args = (
        s_in, a_in, left, lrem, lcol, relax, wall_table, drag_weights, cell_codes.reshape(4, 128),
        wall_mask.reshape(4, 128), recv_xe,
    )
    res_s, res_a = call(
        interior_kernel, par, args, (rowbuf, rowbuf),
        (
            pltpu.VMEM(wall_table.shape, F32), pltpu.VMEM((4, 128), jnp.int32), pltpu.VMEM((4, 128), jnp.int32),
            pltpu.VMEM((16, m), F32), pltpu.VMEM((low, 512), F32), pltpu.VMEM((160, 256), F32),
            pltpu.VMEM((low * step, 512), F32), pltpu.SemaphoreType.DMA((3,)),
        ),
        hbm=(6, 8, 9), us=4.0,
    )
    done, pre = call(
        first_kernel, par,
        (own_e, recv_e, own_n, own_w, recv_xo, recv_xf, res_s, res_a, left, binv), (rowbuf, rowbuf),
    )
    out = sds(s.shape, F32)
    s_next, a_next = call(
        last_kernel, par, (own_n, own_w, recv_n, recv_w, recv_z, pre, comp, done), (out, out),
        (pltpu.VMEM(s.shape, F32), pltpu.VMEM(s.shape, F32), pltpu.SemaphoreType.DMA((2,))), outs_hbm=True,
    )
    return s_next.reshape(state.shape), a_next.reshape(adjoint.shape)


def solution(mesh):
    field, cells = P(None, None, "gy", "gx"), P(None, "gy", "gx")
    in_specs = (field, field, P(), P(), P(), P(), P(), P(), P(), cells, cells)
    return jax.shard_map(
        on_device, mesh=mesh, in_specs=in_specs, out_specs=(field, field), check_vma=False
    )
```

```python
import jax
import jax.numpy as jnp
from jax import lax
from jax.experimental import pallas as pl
from jax.experimental.pallas import tpu as pltpu
from jax.sharding import PartitionSpec as P


F32 = jnp.float32
BF16 = jnp.bfloat16
DIRECT = 368


def both_ways(pairs):
    return [(i, j) for i, j in pairs] + [(j, i) for i, j in pairs]


def split(x):
    hi = x.astype(BF16)
    lo = (x - hi.astype(F32)).astype(BF16)
    return hi, lo


def dot(a, b):
    return lax.dot_general(a, b, (((1,), (0,)), ((), ())), preferred_element_type=F32)


def up16(n):
    return (n + 15) // 16 * 16


def dot3(left, b, m):
    high = up16(m)
    both = dot(left, b[0])
    return both[0:m, :] + (both[high : high + m, :] + dot(left[0:m, :], b[1]))


def dot3_tail(left, rem, b, m):
    tail = jnp.concatenate([b[256:m], jnp.zeros((32 - (m - 256), b.shape[1]), F32)], axis=0)
    hi, lo = split(tail)
    right = jnp.concatenate([hi, hi, lo, jnp.zeros_like(hi)], axis=0)
    return dot3(left[:, 0:256], split(b[0:256]), m) + dot(rem, right)


def fetch(pairs, sems):
    copies = [pltpu.make_async_copy(src, dst, sems.at[i]) for i, (src, dst) in enumerate(pairs)]
    for c in copies:
        c.start()
    return copies


def block(ref, z, y):
    return ref[pl.ds(2 * z + y, ref.shape[0] // 4, stride=4), :]


def fold(x, rows):
    return sum(pltpu.roll(x[g * rows : (g + 1) * rows], 32 * g, 1) if g else x[0:rows] for g in range(4))


def unfold(x, m):
    groups = [pltpu.roll(x, 128 - 32 * g, 1) if g else x for g in range(4)]
    return jnp.concatenate(groups, axis=0)[0:m]


def pack_kernel(par_ref, s_hbm, a_hbm, e_ref, n_ref, w_ref, x_ref, s_ref, a_ref, sems):
    m, half = s_ref.shape[0] // 4, e_ref.shape[0] // 2
    direct = n_ref.shape[0]
    py = par_ref[0] & 1
    copies = fetch([(s_hbm, s_ref), (a_hbm, a_ref)], sems)
    lanes = lax.broadcasted_iota(jnp.int32, (m, 128), 1)
    ends = jnp.zeros((m, 128), F32)
    for f, ref in enumerate((s_ref, a_ref)):
        copies[f].wait()
        for z in range(2):
            cells = pl.ds(z * 128, 128)
            rows = [block(ref, z, y) for y in range(2)]
            e_ref[pl.ds(f * half, m), cells] = jnp.where(py == 0, rows[1], rows[0])
            other = jnp.where(py == 0, rows[0], rows[1])
            near = min(m, direct - f * half)
            n_ref[pl.ds(f * half, near), cells] = other[0:near]
            if near < m:
                w_ref[0 : m - near, cells] = other[near:]
            for y in range(2):
                j = f * 4 + 2 * z + y
                ends = jnp.where((lanes >> 1) == j, pltpu.roll(rows[y], 2 * j + 1, 1), ends)
    rows = x_ref.shape[0]
    x_ref[...] = fold(jnp.concatenate([ends, jnp.zeros((4 * rows - m, 128), F32)], axis=0), rows)


def merge_kernel(par_ref, own_ref, other_ref, out_ref):
    out_ref[...] = own_ref[...] + pltpu.roll(other_ref[...], 16, 1)


def prep_kernel(
    par_ref, s_hbm, a_hbm, up_ref, un_ref, b_hbm, col_ref,
    s_ref, a_ref, left_ref, lrem_ref, binv_ref, comp_ref, lcol_ref, tail_ref,
    b_ref, pad_ref, rem_ref, cmat_ref, sems,
):
    m = b_ref.shape[0]
    high = up16(m)
    low = col_ref.shape[0]
    step = (low + 7) // 8 * 8
    row = par_ref[0] & 1
    copies = fetch(
        [(b_hbm, b_ref), (s_hbm, s_ref), (a_hbm, a_ref)], sems
    )
    rem_ref[...] = jnp.zeros_like(rem_ref)
    cmat_ref[...] = jnp.zeros_like(cmat_ref)
    meets = []
    for f in range(2):
        mats = [up_ref[0], un_ref[0], up_ref[2] - un_ref[2], up_ref[1], un_ref[1]]
        if f == 1:
            mats = [x.T for x in mats]
        for i, x in enumerate(mats):
            hi, lo = split(x)
            left_ref[5 * f + i, 0:m, :] = hi
            left_ref[5 * f + i, high : high + m, :] = lo
            rem_ref[f, 0:m, 32 * i : 32 * i + m - 256] = hi[:, 256:].astype(F32)
            rem_ref[f, high : high + m, 32 * i : 32 * i + m - 256] = lo[:, 256:].astype(F32)
        lrem_ref[f] = rem_ref[f].astype(BF16)
        meets.append(jnp.where((row == 0) == (f == 0), mats[3], mats[4]))
    pad_ref[...] = jnp.zeros_like(pad_ref)

    def keep_tail(at, hi, lo):
        pad_ref[:, 0 : m - 256] = hi[:, 256:].astype(F32)
        pad_ref[:, 32 : 32 + m - 256] = lo[:, 256:].astype(F32)
        pad_ref[:, 64 : 64 + m - 256] = hi[:, 256:].astype(F32)
        tail_ref[at] = pad_ref[...].astype(BF16)

    for f in range(2):
        for i in range(2):
            keep_tail(2 * f + i, left_ref[5 * f + 3 + i, 0:m, :], left_ref[5 * f + 3 + i, high : high + m, :])
    copies[0].wait()
    for f in range(2):
        hi, lo = split(b_ref[...] if f == 0 else b_ref[...].T)
        binv_ref[f, 0:m, :] = hi
        binv_ref[f, high : high + m, :] = lo
        keep_tail(4 + f, hi, lo)
        scale = jnp.where((row == 1) == (f == 0), -0.5, 0.5).astype(F32)
        hi, lo = split(scale * dot3(binv_ref[f], split(meets[f]), m))
        comp_ref[f, 0:m, :] = hi
        comp_ref[f, high : high + m, :] = lo
        keep_tail(6 + f, hi, lo)
    for k in range(low):
        c = col_ref[k]
        c = c + c.T
        c_hi = c.astype(BF16).astype(F32)
        at = pl.ds(k * step, low)
        cmat_ref[at, 0:low] = c_hi
        cmat_ref[at, step : step + low] = c_hi
        cmat_ref[at, 2 * step : 2 * step + low] = (c - c_hi).astype(BF16).astype(F32)
    lcol_ref[...] = cmat_ref[...].astype(BF16)
    copies[1].wait()
    copies[2].wait()


def interior_kernel(
    par_ref, s_ref, a_ref, left_ref, lrem_ref, lcol_ref, relax_ref, wt_hbm, dw_ref, codes_hbm, mask_hbm, xe_ref,
    rs_ref, ra_ref, wt_ref, codes_ref, mask_ref, tab_ref, gain_ref, rrem_ref, u_ref, sems,
):
    m = rs_ref.shape[1]
    low = gain_ref.shape[0]
    step = (low + 7) // 8 * 8
    px = (par_ref[0] >> 1) & 1
    copies = fetch([(codes_hbm, codes_ref), (mask_hbm, mask_ref), (wt_hbm, wt_ref)], sems)
    lanes = lax.broadcasted_iota(jnp.int32, (m, 128), 1)

    def wide(blocks):
        return jnp.concatenate(blocks, axis=1)

    tab_ref[...] = jnp.zeros_like(tab_ref)
    rrem_ref[...] = jnp.zeros_like(rrem_ref)

    def low_of(ref):
        return wide([ref[pl.ds(2 * z + y, low, stride=4), :] for y in range(2) for z in range(2)])

    s_low, a_low = low_of(s_ref), low_of(a_ref)
    s_hi = s_low.astype(BF16).astype(F32)
    s_lo = (s_low - s_hi).astype(BF16).astype(F32)
    gap = jnp.zeros((step - low, 512), F32)
    right = jnp.concatenate([s_hi, gap, s_lo, gap, s_hi, gap, jnp.zeros((128 - 3 * step, 512), F32)], axis=0).astype(BF16)
    u_ref[...] = dot(lcol_ref[...], right)
    adgain = jnp.zeros((low, 512), F32)
    for k in range(low):
        u = u_ref[pl.ds(k * step, low), :]
        adgain = adgain + a_low[k : k + 1, :] * u
        gain_ref[k : k + 1, :] = 0.5 * jnp.sum(s_low * u, axis=0, keepdims=True)
    gain = gain_ref[...]

    for c in copies:
        c.wait()
    tab_ref[0, :] = relax_ref[...]
    tab_ref[1:4, :] = wt_ref[...]
    tab_ref[4, :] = dw_ref[...]
    tab_hi = tab_ref[0:8, :].astype(BF16).astype(F32)
    tab_ref[8:16, :] = tab_ref[0:8, :] - tab_hi
    tab_ref[0:8, :] = tab_hi
    table = tab_ref[...].T.astype(BF16)
    sub = lax.broadcasted_iota(jnp.int32, (16, 128), 0) & 7

    def picked(where_row):
        return dot(table, wide([jnp.where(w, 1.0, 0.0) for w in where_row]).astype(BF16))

    codes = [codes_ref[q : q + 1, :] for q in range(4)]
    walls = [mask_ref[q : q + 1, :] for q in range(4)]
    damp = [
        picked([(sub == 0) | ((sub > 0) & (sub < 4) & (codes[2 * z + y] == sub)) for z in range(2)]) for y in range(2)
    ]
    source = [picked([(sub == 4) & (walls[2 * z + y] != 0) for z in range(2)]) for y in range(2)]

    ends = unfold(xe_ref[...], m)
    ends = jnp.where(px == 0, ends, pltpu.roll(ends, 2, 1))
    for f, (ref, out_ref) in enumerate(((s_ref, rs_ref), (a_ref, ra_ref))):
        sign = 1.0 if f == 0 else -1.0
        blk = [[block(ref, z, y) for z in range(2)] for y in range(2)]
        step_y = wide([sign * (blk[1][z] - blk[0][z]) for z in range(2)])
        for y in range(2):
            bs, hs = [], []
            for z in range(2):
                j = f * 4 + 2 * z + y
                b = blk[y][z]
                end = pltpu.roll(ends, 126 - 2 * j, 1)
                xm = jnp.where(lanes == 0, jnp.where(px == 1, end, 0.0), pltpu.roll(b, 1, 1))
                xp = jnp.where(lanes == 127, jnp.where(px == 0, end, 0.0), pltpu.roll(b, 127, 1))
                bs.append(sign * (b - xm))
                hs.append(sign * (xp - b))
            behind, ahead = wide(bs), wide(hs)
            dz = blk[y][0] - blk[y][1]
            rights = [behind if f == 0 else ahead, ahead if f == 0 else behind, wide([dz, -dz]), step_y]
            use = 4 if (y == 0) == (f == 0) else 3
            total = damp[y] * wide(blk[y])
            if f == 1:
                total = total - source[y]
            for i, r in enumerate(rights):
                k = use if i == 3 else i
                total = total + dot3(left_ref[5 * f + k, :, 0:256], split(r[0:256]), m)
                rrem_ref[32 * k : 32 * k + m - 256, :] = r[256:m]
            idle = 7 - use
            rrem_ref[32 * idle : 32 * idle + 32, :] = jnp.zeros((32, 256), F32)
            out_ref[y] = total + dot3(lrem_ref[f], split(rrem_ref[...]), m)
            g = gain if f == 0 else adgain
            out_ref[y, 0:low, :] = out_ref[y, 0:low, :] - g[:, y * 256 : (y + 1) * 256]


def first_kernel(
    par_ref, own_ref, recv_ref, n_ref, w_ref, xo_ref, xf_ref, rs_ref, ra_ref, left_ref, binv_ref, tail_ref, out_ref, pre_ref,
):
    m, half = rs_ref.shape[1], own_ref.shape[0] // 2
    high = up16(m)
    py, px = par_ref[0] & 1, (par_ref[0] >> 1) & 1
    row = 1 - py
    outer = par_ref[0] >> 2
    lanes = lax.broadcasted_iota(jnp.int32, (m, 128), 1)
    came = jnp.where(outer == 1, pltpu.roll(xf_ref[...], 112, 1), xo_ref[...])
    hi, lo = split(jnp.where(lanes < 16, unfold(came, m), 0.0))
    cols = (hi.astype(F32) + pltpu.roll(lo.astype(F32), 16, 1)).astype(BF16)
    edge = lanes == jnp.where(px == 0, 0, 127)
    near = n_ref.shape[0] - half
    own_o = [n_ref[0:m, :], jnp.concatenate([n_ref[half:, :], w_ref[0 : m - near, :]], axis=0)]
    for f in range(2):
        both = dot(left_ref[5 * f + (px if f == 0 else 1 - px)], cols)
        fix = both[0:m] + (pltpu.roll(both[0:m], 112, 1) + both[high : high + m])
        fix = jnp.where(px == 0, pltpu.roll(fix, 2, 1), fix) * jnp.where((px == 0) == (f == 0), -1.0, 1.0).astype(F32)
        ref = rs_ref if f == 0 else ra_ref
        fixes = [[pltpu.roll(fix, 126 - 2 * (f * 4 + 2 * z + y), 1) for y in range(2)] for z in range(2)]

        def fixed(at):
            return jnp.concatenate(
                [
                    ref[at, :, z * 128 : (z + 1) * 128]
                    + jnp.where(edge, jnp.where(at == 0, fixes[z][0], fixes[z][1]), 0.0)
                    for z in range(2)
                ],
                axis=1,
            )

        own = own_ref[f * half : f * half + m, :]
        gap = recv_ref[f * half : f * half + m, :] - own
        gap = gap * jnp.where((row == 1) == (f == 0), 1.0, -1.0).astype(F32)
        meet = 3 + row if f == 0 else 4 - row
        total = fixed(row) + dot3_tail(left_ref.at[5 * f + meet], tail_ref[2 * f + meet - 3], gap, m)
        out_ref[f] = own - 0.5 * dot3_tail(binv_ref.at[f], tail_ref[4 + f], total, m)
        pre_ref[f] = own_o[f] - 0.5 * dot3_tail(binv_ref.at[f], tail_ref[4 + f], fixed(py), m)


def last_kernel(
    par_ref, n_ref, w_ref, recv_n_ref, recv_w_ref, recv_z_ref, pre_ref, comp_ref, tail_ref, done_ref, s_hbm, a_hbm,
    s_ref, a_ref, sems,
):
    m, direct = pre_ref.shape[1], n_ref.shape[0]
    half = (m + 7) // 8 * 8
    row, outer = par_ref[0] & 1, par_ref[0] >> 2
    near = direct - half
    copies = [pltpu.make_async_copy(s_ref, s_hbm, sems.at[0]), pltpu.make_async_copy(a_ref, a_hbm, sems.at[1])]
    for f, ref in enumerate((s_ref, a_ref)):
        if f == 0:
            gap = recv_n_ref[0:m, :] - n_ref[0:m, :]
        else:
            relayed = jnp.where(outer == 1, recv_z_ref[...], recv_w_ref[...]) - w_ref[...]
            gap = jnp.concatenate([recv_n_ref[half:, :] - n_ref[half:, :], relayed[0 : m - near]], axis=0)
        new = pre_ref[f] + dot3_tail(comp_ref.at[f], tail_ref[6 + f], gap, m)
        for z in range(2):
            here = new[:, z * 128 : (z + 1) * 128]
            there = done_ref[f, :, z * 128 : (z + 1) * 128]
            ref[pl.ds(2 * z, m, stride=4), :] = jnp.where(row == 0, here, there)
            ref[pl.ds(2 * z + 1, m, stride=4), :] = jnp.where(row == 0, there, here)
        copies[f].start()
    for c in copies:
        c.wait()


def whole(shape):
    return pl.BlockSpec(shape, lambda *_: (0,) * len(shape))


IN_HBM = pl.BlockSpec(memory_space=pltpu.HBM)


def call(kernel, scalars, args, outs, scratch=(), hbm=(), us=1.0, outs_hbm=False):
    in_specs = [IN_HBM if i in hbm else whole(x.shape) for i, x in enumerate(args)]
    args = [pltpu.with_memory_space_constraint(x, pltpu.HBM) if i in hbm else x for i, x in enumerate(args)]
    return pl.pallas_call(
        kernel,
        out_shape=outs,
        grid_spec=pltpu.PrefetchScalarGridSpec(
            num_scalar_prefetch=1,
            grid=(1,),
            in_specs=in_specs,
            out_specs=jax.tree.map(lambda o: IN_HBM if outs_hbm else whole(o.shape), outs),
            scratch_shapes=list(scratch),
        ),
        compiler_params=pltpu.CompilerParams(vmem_limit_bytes=36 * 1024 * 1024),
        cost_estimate=pl.CostEstimate(flops=int(us * 5e8), bytes_accessed=int(us * 1e6), transcendentals=0),
    )(scalars, *args)


def on_device(
    state, adjoint, upwind_pos, upwind_neg, collision, relax, wall_table, drag_weights, block_inverse,
    cell_codes, wall_mask,
):
    m, low = state.shape[0], collision.shape[0]
    half = (m + 7) // 8 * 8
    high, step = up16(m), (low + 7) // 8 * 8
    gy, gx = lax.axis_index("gy"), lax.axis_index("gx")
    ny, nx = lax.axis_size("gy"), lax.axis_size("gx")
    px = gx & 1
    spot = gy & 3
    outer = 1 - ((spot ^ (spot >> 1)) & 1)
    par = ((gy & 1) + 2 * px + 4 * outer).astype(jnp.int32).reshape(1)
    s = state.reshape(m * 4, 128)
    a = adjoint.reshape(m * 4, 128)
    sds = jax.ShapeDtypeStruct
    rowbuf = sds((2, m, 256), F32)
    colbuf = sds(((m + 31) // 32 * 8, 128), F32)
    relayed = 2 * half - DIRECT
    own_e, own_n, own_w, ends = call(
        pack_kernel, par, (s, a),
        (sds((2 * half, 256), F32), sds((DIRECT, 256), F32), sds((relayed, 256), F32), colbuf),
        (pltpu.VMEM(s.shape, F32), pltpu.VMEM(s.shape, F32), pltpu.SemaphoreType.DMA((2,))),
        hbm=(0, 1),
    )
    even = lambda n: both_ways([(i, i + 1) for i in range(0, n - 1, 2)])
    odd = lambda n: both_ways([(i, i + 1) for i in range(1, n - 1, 2)])
    quads = range(0, ny, 4)
    around = both_ways([(q, q + 3) for q in quads] + [(q + 1, q + 2) for q in quads])
    onward = [(q, q + 4) for q in quads if q + 4 < ny] + [(q + 7, q + 3) for q in quads if q + 4 < ny]
    recv_n = lax.ppermute(own_n, "gy", odd(ny))
    recv_w = lax.ppermute(own_w, "gy", around)
    recv_e = lax.ppermute(own_e, "gy", even(ny))
    recv_xe = lax.ppermute(ends, "gx", even(nx))
    ends_p = lax.ppermute(ends, "gy", even(ny))
    ends_m = call(merge_kernel, par, (ends, ends_p), colbuf)
    inner = [g for g in range(ny) if g % 4 in (1, 2)]
    recv_xo = lax.ppermute(ends_m, ("gx", "gy"), [(i * ny + g, j * ny + g) for i, j in odd(nx) for g in inner])
    recv_xf = lax.ppermute(recv_xo, "gy", even(ny))
    recv_z = lax.ppermute(recv_w, "gy", onward)
    args = (s, a, upwind_pos, upwind_neg, block_inverse, collision)
    weights = lambda n, k: sds((n, 2 * high, k), BF16)
    s_in, a_in, left, lrem, binv, comp, lcol, tails = call(
        prep_kernel, par, args,
        (
            sds(s.shape, F32), sds(a.shape, F32), weights(10, m), weights(2, 160), weights(2, m), weights(2, m),
            sds((low * step, 128), BF16), sds((8, m, 128), BF16),
        ),
        (
            pltpu.VMEM((m, m), F32), pltpu.VMEM((m, 128), F32), pltpu.VMEM((2, 2 * high, 160), F32), pltpu.VMEM((low * step, 128), F32), pltpu.SemaphoreType.DMA((3,)),
        ),
        hbm=(0, 1, 4), us=3.0,
    )
    args = (
        s_in, a_in, left, lrem, lcol, relax, wall_table, drag_weights, cell_codes.reshape(4, 128),
        wall_mask.reshape(4, 128), recv_xe,
    )
    res_s, res_a = call(
        interior_kernel, par, args, (rowbuf, rowbuf),
        (
            pltpu.VMEM(wall_table.shape, F32), pltpu.VMEM((4, 128), jnp.int32), pltpu.VMEM((4, 128), jnp.int32),
            pltpu.VMEM((16, m), F32), pltpu.VMEM((low, 512), F32), pltpu.VMEM((160, 256), F32),
            pltpu.VMEM((low * step, 512), F32), pltpu.SemaphoreType.DMA((3,)),
        ),
        hbm=(6, 8, 9), us=4.0,
    )
    done, pre = call(
        first_kernel, par,
        (own_e, recv_e, own_n, own_w, recv_xo, recv_xf, res_s, res_a, left, binv, tails), (rowbuf, rowbuf),
    )
    out = sds(s.shape, F32)
    s_next, a_next = call(
        last_kernel, par, (own_n, own_w, recv_n, recv_w, recv_z, pre, comp, tails, done), (out, out),
        (pltpu.VMEM(s.shape, F32), pltpu.VMEM(s.shape, F32), pltpu.SemaphoreType.DMA((2,))), outs_hbm=True,
    )
    return s_next.reshape(state.shape), a_next.reshape(adjoint.shape)


def solution(mesh):
    field, cells = P(None, None, "gy", "gx"), P(None, "gy", "gx")
    in_specs = (field, field, P(), P(), P(), P(), P(), P(), P(), cells, cells)
    return jax.shard_map(
        on_device, mesh=mesh, in_specs=in_specs, out_specs=(field, field), check_vma=False
    )
```
